128 devices in a mesh: phi: 8 (over x, core), eta: 16 (over z, y).
Axes of the slice: x: 4, y: 4, z: 4, core: 2. Of those that a mesh axis runs over, the one named last changes fastest.
Arguments:
- query: bfloat16 [192, 65536], P(None, ('phi', 'eta')), may hold values from -64 to 64
- key_rows: bfloat16 [192, 65536], P(None, ('phi', 'eta')), may hold values from -6 to 6
- value: bfloat16 [192, 65536], P(None, ('phi', 'eta')), may hold values from -6 to 6
- out_grad: bfloat16 [192, 65536], P(None, ('phi', 'eta')), may hold values from -6 to 6
- members: int32 [3, 512, 128], P(None, ('phi', 'eta')), may hold values from 0 to 65535, as said below
Outputs:
- query_grad: bfloat16 [192, 65536], P(None, ('phi', 'eta'))
- key_grad: bfloat16 [192, 65536], P(None, ('phi', 'eta'))
- value_grad: bfloat16 [192, 65536], P(None, ('phi', 'eta'))
The draws below stay inside these ranges and needn't reach their ends.
Inputs may be any that keep to these rules, and one draw needn't show every extreme that they name: `members`: bucket i of every table is owned by device i // 4 in the order phi+eta, and point id j lies on device j // 512. In each table every point id appears exactly once. In one table a device's buckets hold at most 5 points of any one source device, and exactly 5 for some pairs of devices.
All inputs are finite; a program needn't handle non-finite values.
Results may differ from the reference program's by a relative error of at most 0.0097.
Values may be sent and summed in bfloat16 or wider, within the bound.
A program may use at most 64 MiB of HBM per device.

```python
import jax
import jax.numpy as jnp
from jax import lax

HEADS = 8
HEAD_DIM = 24
FEAT = 192
TABLES = 3
BUCKET = 128
P_DEV = 512
OWNERS = 128
POINTS = 65536
BUCK_DEV = 4
NBUCK = 512
CAP = 5


def member_table(key):
    key_one, key_two, key_three = jax.random.split(key, 3)
    offsets = jax.random.permutation(key_one, OWNERS).astype(jnp.int32)
    device_no = jnp.arange(OWNERS, dtype=jnp.int32)
    quarter = OWNERS // 4
    base_count = P_DEV // OWNERS
    weights = jnp.where(device_no < quarter, CAP, jnp.where(device_no < 2 * quarter, base_count - base_count // 4, base_count)).astype(jnp.int32)
    ending = jnp.cumsum(weights).astype(jnp.int32)
    position = jnp.arange(P_DEV, dtype=jnp.int32)
    section_of = jnp.sum((ending[None, :] <= position[:, None]).astype(jnp.int32), axis=1)
    source = (device_no[:, None] - offsets[section_of][None, :]) % OWNERS
    shuffle = jax.vmap(lambda subkey: jax.random.permutation(subkey, P_DEV))(jax.random.split(key_two, OWNERS)).astype(jnp.int32)
    local_ids = shuffle[source, position[None, :]]
    point_ids = source * P_DEV + local_ids
    placing = jax.vmap(lambda subkey: jax.random.permutation(subkey, P_DEV))(jax.random.split(key_three, OWNERS)).astype(jnp.int32)
    point_ids = jnp.take_along_axis(point_ids, placing, axis=1)
    return point_ids.reshape(NBUCK, BUCKET).astype(jnp.int32)


def draw_members(key, part):
    return jnp.stack([member_table(jax.random.fold_in(key, table_no)) for table_no in range(TABLES)])


def draw_query(key, part):
    key_one = jax.random.fold_in(key, 0)
    sample = jnp.clip(jax.random.normal(key_one, (FEAT, POINTS), jnp.float32), -6.0, 6.0)
    return sample.astype(jnp.bfloat16)


def levels(key, shape, shards, low, high):
    def one(dim, blocks):
        draws = jax.random.uniform(jax.random.fold_in(jax.random.fold_in(key, 6), dim), (blocks,), jnp.float32, low / len(shards), high / len(shards))
        return jnp.repeat(jnp.exp(draws), shape[dim] // blocks).reshape((-1,) + (1,) * (len(shape) - dim - 1))

    loudness = one(*shards[0])
    for cut in shards[1:]:
        loudness = loudness * one(*cut)
    return loudness


def noise(key, extent, deviation, bound, cuts=(), kind=jnp.bfloat16):
    entries = deviation * jax.random.normal(key, extent, jnp.float32)
    if cuts:
        entries = entries * levels(key, extent, cuts, -0.22, 0.18)
    return jnp.clip(entries, -bound, bound).astype(kind)


def setup_inputs(seed: int = 0) -> dict:
    arg_keys = jax.random.split(jax.random.key(seed), 6)
    return {
        "query": draw_query(jax.random.fold_in(arg_keys[5], 71), 0),
        "key_rows": noise(arg_keys[1], (FEAT, POINTS), 1.0, 6.0, ((1, 128),)),
        "value": noise(arg_keys[2], (FEAT, POINTS), 1.0, 6.0, ((1, 128),)),
        "out_grad": noise(arg_keys[3], (FEAT, POINTS), 1.0, 6.0, ((1, 128),)),
        "members": draw_members(jax.random.fold_in(arg_keys[5], 71), 0),
    }


def bucket_grads(query_part, key_part, value_part, grad_part):
    scale = HEAD_DIM ** -0.5
    query_full = query_part.astype(jnp.float32)
    key_full = key_part.astype(jnp.float32)
    value_full = value_part.astype(jnp.float32)
    grad_full = grad_part.astype(jnp.float32)
    dots = jnp.einsum('bihd,bjhd->bhij', query_full, key_full)
    key_norm = jnp.einsum('bjhd,bjhd->bhj', key_full, key_full)
    scores = scale * (dots - 0.5 * key_norm[:, :, None, :])
    row_max = jnp.max(scores, axis=-1, keepdims=True)
    expons = jnp.exp(scores - row_max)
    probs = expons / jnp.sum(expons, axis=-1, keepdims=True)
    probs_low = probs.astype(jnp.bfloat16).astype(jnp.float32)
    outputs = jnp.einsum('bhij,bjhd->bihd', probs_low, value_full)
    delta = jnp.sum(grad_full * outputs, axis=-1)
    dprob = jnp.einsum('bihd,bjhd->bhij', grad_full, value_full)
    dscore = scale * probs * (dprob - jnp.transpose(delta, (0, 2, 1))[..., None])
    dscore_low = dscore.astype(jnp.bfloat16).astype(jnp.float32)
    query_grad = jnp.einsum('bhij,bjhd->bihd', dscore_low, key_full)
    column_sums = jnp.transpose(jnp.sum(dscore, axis=2), (0, 2, 1))[..., None]
    key_grad = jnp.einsum('bhij,bihd->bjhd', dscore_low, query_full) - column_sums * key_full
    value_grad = jnp.einsum('bhij,bihd->bjhd', probs_low, grad_full)
    shape_rows = (query_part.shape[0], query_part.shape[1], HEADS * HEAD_DIM)
    return jnp.concatenate([query_grad.reshape(shape_rows).astype(jnp.bfloat16),
                            key_grad.reshape(shape_rows).astype(jnp.bfloat16),
                            value_grad.reshape(shape_rows).astype(jnp.bfloat16)], axis=-1)


def reference(query, key_rows, value, out_grad, members):
    width = HEADS * HEAD_DIM
    query_rows = query.T
    key_points = key_rows.T
    value_rows = value.T
    grad_rows = out_grad.T
    summed = jnp.zeros((POINTS, 3 * width), jnp.float32)
    for table_no in range(TABLES):
        group_ids = members[table_no].reshape(OWNERS, BUCK_DEV, BUCKET).astype(jnp.int32)

        def one_group(bucket_ids):
            shape_heads = (BUCK_DEV, BUCKET, HEADS, HEAD_DIM)
            return bucket_grads(query_rows[bucket_ids].reshape(shape_heads), key_points[bucket_ids].reshape(shape_heads),
                                value_rows[bucket_ids].reshape(shape_heads), grad_rows[bucket_ids].reshape(shape_heads))

        gradient = lax.map(one_group, group_ids)
        summed = summed.at[group_ids.reshape(-1)].add(gradient.reshape(-1, 3 * width).astype(jnp.float32))
    result = summed.astype(jnp.bfloat16).T
    return (result[:width], result[width:2 * width], result[2 * width:])
```

```python
import functools

import jax
import jax.numpy as jnp
from jax import lax
from jax.experimental import pallas as pl
from jax.experimental.pallas import tpu as pltpu
from jax.sharding import PartitionSpec as P

HEADS = 8
HEAD_DIM = 24
TABLES = 3
BUCKET = 128
BUCKETS = 12
POINTS = 512
OWNERS = 128
CAP = 5
SLOT = 16
ROWS = OWNERS * SLOT
GROUPS = 2
GH = HEADS // GROUPS
GF = GH * HEAD_DIM
WIDE = 4 * GF
BACK = (256, 384)
CHUNK = 256
STEP_MUL = 37
STEP_INV = 45
MESH = pl.DeviceIdType.MESH
F32 = jnp.float32
BF16 = jnp.bfloat16


def dot(a, b):
    return jnp.dot(a, b, preferred_element_type=F32)


def iota(shape, dim):
    return lax.broadcasted_iota(jnp.int32, shape, dim)


def place():
    phi, eta = lax.axis_index("phi"), lax.axis_index("eta")
    return phi // 2, phi % 2, eta // 4, eta % 4


def peer(step, sign):
    x, core, z, y = place()
    shift = (step * STEP_MUL) % OWNERS
    px = (x + sign * (shift // 32) + 4) % 4
    pc = (core + (shift // 16) % 2) % 2
    pz = (z + sign * ((shift // 4) % 4) + 4) % 4
    py = (y + sign * (shift % 4) + 4) % 4
    return (px * 2 + pc, pz * 4 + py)


def onehot(mask):
    return jnp.where(mask, 1.0, 0.0).astype(BF16)


def kernel(
    query_ref, key_ref, value_ref, grad_ref, members_ref,
    query_out, key_out, value_out,
    columns, wanted, requests, points0, points1, pick, pick_t, gather, gather_t,
    out0, out1, in0, in1, tiles, grads0, grads1, back0, back1, home0, home1,
    send_sem, recv_sem,
):
    points_in, outs, ins = (points0, points1), (out0, out1), (in0, in1)
    grads, backs, homes = (grads0, grads1), (back0, back1), (home0, home1)

    def copy(src, dst, step, sign, number):
        return pltpu.make_async_remote_copy(
            src_ref=src, dst_ref=dst, send_sem=send_sem.at[number], recv_sem=recv_sem.at[number],
            device_id=peer(step, sign), device_id_type=MESH,
        )

    def wait_all(ref, sem):
        pltpu.make_async_copy(ref, ref, sem).wait()

    barrier = pltpu.get_barrier_semaphore()

    @pl.loop(1, OWNERS)
    def _(step):
        pl.semaphore_signal(barrier, inc=1, device_id=peer(step, 1), device_id_type=MESH)

    x, core, z, y = place()
    ids = jnp.concatenate([members_ref[t] for t in range(TABLES)] + [jnp.zeros((4, 128), jnp.int32)], axis=0)
    source, local = ids >> 9, ids & 511
    shift = (
        (((x - (source >> 5)) & 3) << 5)
        | (((core - (source >> 4)) & 1) << 4)
        | (((z - (source >> 2)) & 3) << 2)
        | ((y - source) & 3)
    )
    step_of = (shift * STEP_INV) & (OWNERS - 1)
    both = (step_of * 1024 + local).astype(F32)
    columns[...] = jnp.transpose(jnp.concatenate([both, jnp.zeros((112, 128), F32)], axis=0))
    lane = iota((128, 128), 1)
    sub = iota((128, 128), 0)
    below = onehot(lane < sub)
    asked = jnp.zeros((128, 128), F32)
    codes = jnp.zeros((128, 128), F32)
    for t in range(TABLES):
        seen = jnp.zeros((1, 128), F32)
        for b in range(4):
            n = 4 * t + b
            column = columns[:, n : n + 1].astype(jnp.int32)
            step_col, ask = column >> 10, (column & 1023) + 1
            mine = lane == step_col
            mine_f = jnp.where(mine, 1.0, 0.0)
            earlier = dot(below, mine_f.astype(BF16)) + seen
            rank = jnp.sum(jnp.where(mine, earlier, 0.0), axis=1, keepdims=True).astype(jnp.int32)
            seen = seen + jnp.sum(mine_f, axis=0, keepdims=True)
            slot = CAP * t + rank
            asks = jnp.where(lane == slot, ask >> 4, 0) + jnp.where(lane == slot + SLOT, ask & 15, 0)
            mine_t = onehot(sub == step_of[n : n + 1, :])
            asked = asked + dot(mine_t, asks.astype(F32).astype(BF16))
            codes = jnp.where(lane == n, (SLOT * step_col + slot).astype(F32), codes)
    wanted[...] = asked
    columns[...] = codes
    codes_t = jnp.transpose(codes).astype(jnp.int32)

    pl.semaphore_wait(barrier, OWNERS - 1)

    @pl.loop(1, OWNERS)
    def _(step):
        copy(wanted.at[pl.ds(step, 1)], requests.at[pl.ds(step, 1)], step, -1, 0).start()

    requests[pl.ds(0, 1), :] = asked[0:1, :]
    for g in range(GROUPS):
        rows = pl.ds(g * GF, GF)
        stacked = jnp.concatenate([r[rows, :] for r in (query_ref, key_ref, value_ref, grad_ref)], axis=0)
        points_in[g][...] = jnp.transpose(stacked)
    wait_all(requests.at[pl.ds(1, OWNERS - 1)], recv_sem.at[0])

    asked_low = requests[...].astype(BF16)
    chunk_row = iota((CHUNK, 128), 0)
    chunk_lane = iota((CHUNK, 128), 1)
    weight = jnp.where(chunk_lane == chunk_row % SLOT, 16.0, 0.0) + jnp.where(chunk_lane == chunk_row % SLOT + SLOT, 1.0, 0.0)
    ones = jnp.ones((128, POINTS), BF16)
    number = (iota((CHUNK, POINTS), 1) + 1).astype(F32)

    @pl.loop(0, ROWS // CHUNK)
    def _(k):
        rows = pl.ds(pl.multiple_of(k * CHUNK, CHUNK), CHUNK)
        spread = onehot(chunk_lane == chunk_row // SLOT + k * (CHUNK // SLOT))
        asks = dot(spread, asked_low) * weight
        picked = onehot(dot(asks.astype(BF16), ones) == number)
        pick[rows, :] = picked
        for g in range(GROUPS):
            outs[g][rows, :] = dot(picked, points_in[g][...]).astype(BF16)

    for g in range(GROUPS):

        @pl.loop(1, OWNERS)
        def _(step, g=g):
            rows = pl.ds(pl.multiple_of(step * SLOT, SLOT), SLOT)
            copy(outs[g].at[rows], ins[g].at[rows], step, 1, 1 + g).start()

        ins[g][pl.ds(0, SLOT), :] = outs[g][pl.ds(0, SLOT), :]

    @pl.loop(0, ROWS // CHUNK)
    def _(k):
        rows = pl.ds(pl.multiple_of(k * CHUNK, CHUNK), CHUNK)
        pick_t[:, rows] = jnp.transpose(pick[rows, :])

    for n in range(BUCKETS):
        span = pl.ds(n * BUCKET, BUCKET)
        code = columns[:, n : n + 1].astype(jnp.int32)
        gather[span, :] = onehot(iota((BUCKET, ROWS), 1) == code)
        gather_t[:, span] = onehot(iota((ROWS, BUCKET), 0) == codes_t[n : n + 1, :])

    scale = HEAD_DIM**-0.5
    log2e = 1.4426950408889634
    feature = iota((BUCKET, GF), 1) // HEAD_DIM

    def attend(g, n):
        span = pl.ds(pl.multiple_of(n * BUCKET, BUCKET), BUCKET)
        tile = tiles[span, :]
        full = tile.astype(F32)
        turned = jnp.transpose(full)
        q_low, k_low, v_low, g_low = (tile[:, i * GF : (i + 1) * GF] for i in range(4))
        k_full = full[:, GF : 2 * GF]
        q_t, k_t, v_t, g_t = (turned[i * GF : (i + 1) * GF] for i in range(4))

        def spread_t(part):
            row = iota((GF, BUCKET), 0) // HEAD_DIM
            return jnp.concatenate([jnp.where(row == h, part, 0.0) for h in range(GH)], axis=1).astype(BF16)

        def spread(part):
            return jnp.concatenate([jnp.where(feature == h, part, jnp.zeros_like(part)) for h in range(GH)], axis=0)

        squares = k_full * k_full
        dots = dot(k_low, spread_t(q_t))
        logits = jnp.concatenate(
            [
                dots[:, h * BUCKET : (h + 1) * BUCKET]
                - 0.5 * jnp.sum(jnp.where(feature == h, squares, 0.0), axis=1, keepdims=True)
                for h in range(GH)
            ],
            axis=1,
        )
        top = jnp.max(logits, axis=0, keepdims=True)
        expons = jnp.exp2((logits - top) * (scale * log2e))
        probs = expons * (1.0 / jnp.sum(expons, axis=0, keepdims=True))
        probs_low = probs.astype(BF16)
        dprob = dot(v_low, spread_t(g_t))

        def paired(left, right):
            left = left.astype(BF16)
            parts = []
            for u in range(GH // 2):
                both = dot(left[2 * HEAD_DIM * u : 2 * HEAD_DIM * (u + 1)], right[:, 2 * BUCKET * u : 2 * BUCKET * (u + 1)])
                parts += [both[:HEAD_DIM, :BUCKET], both[HEAD_DIM:, BUCKET:]]
            return parts

        delta = jnp.concatenate(
            [
                jnp.sum(part * g_t[h * HEAD_DIM : (h + 1) * HEAD_DIM], axis=0, keepdims=True)
                for h, part in enumerate(paired(v_t, probs_low))
            ],
            axis=1,
        )
        dscore = scale * probs * (dprob - delta)
        dscore_low = dscore.astype(BF16)
        query_part = jnp.transpose(jnp.concatenate(paired(k_t, dscore_low), axis=0)).astype(BF16)
        sums = jnp.zeros((BUCKET, GF), F32)
        for h in range(GH):
            total = jnp.sum(dscore[:, h * BUCKET : (h + 1) * BUCKET], axis=1, keepdims=True)
            sums = jnp.where(feature == h, total, sums)
        key_part = (dot(dscore_low, spread(q_low)) - sums * k_full).astype(BF16)
        value_part = dot(probs_low, spread(g_low)).astype(BF16)
        if g == 0:
            grads0[span, :] = jnp.concatenate([query_part, key_part, value_part[:, :64]], axis=1)
            grads1[span, 288:320] = value_part[:, 64:]
        else:
            grads1[span, 0:288] = jnp.concatenate([query_part, key_part, value_part], axis=1)

    grads1[:, 256:384] = jnp.zeros((BUCKETS * BUCKET, 128), BF16)
    for g in range(GROUPS):
        wait_all(ins[g].at[pl.ds(SLOT, ROWS - SLOT)], recv_sem.at[1 + g])

        @pl.loop(0, TABLES)
        def _(t, g=g):
            rows = pl.ds(pl.multiple_of(t * POINTS, POINTS), POINTS)
            tiles[rows, :] = dot(gather[rows, :], ins[g][...]).astype(BF16)

        @pl.loop(0, BUCKETS)
        def _(n, g=g):
            attend(g, n)

        @pl.loop(0, ROWS // CHUNK)
        def _(k, g=g):
            rows = pl.ds(pl.multiple_of(k * CHUNK, CHUNK), CHUNK)
            backs[g][rows, :] = dot(gather_t[rows, :], grads[g][...]).astype(BF16)

        @pl.loop(1, OWNERS)
        def _(step, g=g):
            rows = pl.ds(pl.multiple_of(step * SLOT, SLOT), SLOT)
            copy(backs[g].at[rows], homes[g].at[rows], step, -1, 3 + g).start()

        homes[g][pl.ds(0, SLOT), :] = backs[g][pl.ds(0, SLOT), :]

    for g in range(GROUPS):
        wait_all(homes[g].at[pl.ds(SLOT, ROWS - SLOT)], recv_sem.at[3 + g])
        result = jnp.transpose(dot(pick_t[...], homes[g][...])).astype(BF16)
        mine = pl.ds(g * GF, GF)
        query_out[mine, :] = result[0:GF]
        key_out[mine, :] = result[GF : 2 * GF]
        if g == 0:
            value_out[pl.ds(0, 64), :] = result[192:256]
        else:
            value_out[mine, :] = result[192:288]
            value_out[pl.ds(64, 32), :] = result[288:320]

    wait_all(wanted.at[pl.ds(1, OWNERS - 1)], send_sem.at[0])
    for g in range(GROUPS):
        wait_all(outs[g].at[pl.ds(SLOT, ROWS - SLOT)], send_sem.at[1 + g])
        wait_all(backs[g].at[pl.ds(SLOT, ROWS - SLOT)], send_sem.at[3 + g])


def on_device(query, key_rows, value, out_grad, members):
    shape = jax.ShapeDtypeStruct(query.shape, BF16)
    vmem = pl.BlockSpec(memory_space=pltpu.VMEM)
    return pl.pallas_call(
        kernel,
        name="hept_backward",
        out_shape=(shape, shape, shape),
        in_specs=[vmem] * 5,
        out_specs=(vmem,) * 3,
        scratch_shapes=[
            pltpu.VMEM((128, 128), F32),
            pltpu.VMEM((128, 128), F32),
            pltpu.VMEM((128, 128), F32),
            pltpu.VMEM((POINTS, WIDE), BF16),
            pltpu.VMEM((POINTS, WIDE), BF16),
            pltpu.VMEM((ROWS, POINTS), BF16),
            pltpu.VMEM((POINTS, ROWS), BF16),
            pltpu.VMEM((BUCKETS * BUCKET, ROWS), BF16),
            pltpu.VMEM((ROWS, BUCKETS * BUCKET), BF16),
            pltpu.VMEM((ROWS, WIDE), BF16),
            pltpu.VMEM((ROWS, WIDE), BF16),
            pltpu.VMEM((ROWS, WIDE), BF16),
            pltpu.VMEM((ROWS, WIDE), BF16),
            pltpu.VMEM((BUCKETS * BUCKET, WIDE), BF16),
            pltpu.VMEM((BUCKETS * BUCKET, BACK[0]), BF16),
            pltpu.VMEM((BUCKETS * BUCKET, BACK[1]), BF16),
            pltpu.VMEM((ROWS, BACK[0]), BF16),
            pltpu.VMEM((ROWS, BACK[1]), BF16),
            pltpu.VMEM((ROWS, BACK[0]), BF16),
            pltpu.VMEM((ROWS, BACK[1]), BF16),
            pltpu.SemaphoreType.DMA((5,)),
            pltpu.SemaphoreType.DMA((5,)),
        ],
        compiler_params=pltpu.CompilerParams(
            collective_id=0, has_side_effects=True, vmem_limit_bytes=56 * 1024 * 1024
        ),
    )(query, key_rows, value, out_grad, members)


def solution(mesh):
    in_specs = (
        P(None, ("phi", "eta")),
        P(None, ("phi", "eta")),
        P(None, ("phi", "eta")),
        P(None, ("phi", "eta")),
        P(None, ("phi", "eta"), None),
    )
    out_specs = (P(None, ("phi", "eta")), P(None, ("phi", "eta")), P(None, ("phi", "eta")))
    return jax.shard_map(
        on_device, mesh=mesh, in_specs=in_specs, out_specs=out_specs, check_vma=False
    )
```

```python
import functools

import jax
import jax.numpy as jnp
from jax import lax
from jax.experimental import pallas as pl
from jax.experimental.pallas import tpu as pltpu
from jax.sharding import PartitionSpec as P

HEADS = 8
HEAD_DIM = 24
TABLES = 3
BUCKET = 128
BUCKETS = 12
POINTS = 512
OWNERS = 128
CAP = 5
SLOT = 16
ROWS = OWNERS * SLOT
TROWS = OWNERS * CAP
GROUPS = 2
GH = HEADS // GROUPS
GF = GH * HEAD_DIM
WIDE = 4 * GF
BACK = (256, 384)
CHUNK = 256
CHUNKS = ROWS // CHUNK
PER = CHUNK // SLOT
TCHUNK = PER * CAP
TOGETHER = 2
STEP_MUL = 37
STEP_INV = 45
MESH = pl.DeviceIdType.MESH
F32 = jnp.float32
BF16 = jnp.bfloat16


def dot(a, b):
    return jnp.dot(a, b, preferred_element_type=F32)


def iota(shape, dim):
    return lax.broadcasted_iota(jnp.int32, shape, dim)


def place():
    phi, eta = lax.axis_index("phi"), lax.axis_index("eta")
    return phi // 2, phi % 2, eta // 4, eta % 4


def torus():
    x, core, z, y = place()
    xs = [((x + a) % 4) * 2 for a in range(4)]
    cores = [core, 1 - core]
    zs = [((z + a) % 4) * 4 for a in range(4)]
    ys = [(y + a) % 4 for a in range(4)]

    def peer(step, sign):
        shift = (step * STEP_MUL) % OWNERS
        a, c, d = (sign * (shift // n) % 4 for n in (32, 4, 1))
        return (xs[a] + cores[shift // 16 % 2], zs[c] + ys[d])

    return peer


def onehot(mask):
    return jnp.where(mask, 1.0, 0.0).astype(BF16)


def kernel(
    query_any, key_any, value_any, grad_any, members_any,
    query_out, key_out, value_out,
    query_ref, key_ref, value_ref, grad_ref, members_ref,
    columns, wanted, requests, points0, points1, pick, pick_t, gather, gather_t,
    out0, out1, in0, in1, rows_of, tiles, grads0, grads1, slots0, slots1, back0, back1, home0, home1,
    load_sem, send_sem, recv_sem,
):
    points_in, outs, ins = (points0, points1), (out0, out1), (in0, in1)
    grads, slots, backs, homes = (grads0, grads1), (slots0, slots1), (back0, back1), (home0, home1)
    peer = torus()

    def copy(src, dst, step, sign, sent, received):
        return pltpu.make_async_remote_copy(
            src_ref=src, dst_ref=dst, send_sem=send_sem.at[sent], recv_sem=recv_sem.at[received],
            device_id=peer(step, sign), device_id_type=MESH,
        )

    def wait_all(ref, sem):
        pltpu.make_async_copy(ref, ref, sem).wait()

    barrier = pltpu.get_barrier_semaphore()
    loads = [
        pltpu.make_async_copy(src, dst, load_sem.at[i])
        for i, (src, dst) in enumerate(
            [
                (members_any, members_ref),
                (query_any, query_ref),
                (key_any, key_ref),
                (value_any, value_ref),
                (grad_any, grad_ref),
            ]
        )
    ]
    for load in loads:
        load.start()
    for step in range(1, OWNERS):
        pl.semaphore_signal(barrier, inc=1, device_id=peer(step, 1), device_id_type=MESH)
    loads[0].wait()

    x, core, z, y = place()
    ids = jnp.concatenate([members_ref[t] for t in range(TABLES)] + [jnp.zeros((4, 128), jnp.int32)], axis=0)
    source, local = ids >> 9, ids & 511
    shift = (
        (((x - (source >> 5)) & 3) << 5)
        | (((core - (source >> 4)) & 1) << 4)
        | (((z - (source >> 2)) & 3) << 2)
        | ((y - source) & 3)
    )
    step_of = (shift * STEP_INV) & (OWNERS - 1)
    both = (step_of * 1024 + local).astype(F32)
    columns[...] = jnp.transpose(jnp.concatenate([both, jnp.zeros((112, 128), F32)], axis=0))
    lane = iota((128, 128), 1)
    sub = iota((128, 128), 0)
    below = onehot(lane < sub)
    asked = jnp.zeros((128, 128), F32)
    codes = jnp.zeros((128, 128), F32)
    for t in range(TABLES):
        seen = jnp.zeros((1, 128), F32)
        for b in range(4):
            n = 4 * t + b
            column = columns[:, n : n + 1].astype(jnp.int32)
            step_col, ask = column >> 10, (column & 1023) + 1
            mine = lane == step_col
            mine_f = jnp.where(mine, 1.0, 0.0)
            earlier = dot(below, mine_f.astype(BF16)) + seen
            rank = jnp.sum(jnp.where(mine, earlier, 0.0), axis=1, keepdims=True).astype(jnp.int32)
            seen = seen + jnp.sum(mine_f, axis=0, keepdims=True)
            slot = CAP * t + rank
            asks = jnp.where(lane == slot, ask >> 4, 0) + jnp.where(lane == slot + SLOT, ask & 15, 0)
            mine_t = onehot(sub == step_of[n : n + 1, :])
            asked = asked + dot(mine_t, asks.astype(F32).astype(BF16))
            codes = jnp.where(lane == n, (CAP * step_col + rank).astype(F32), codes)
    wanted[...] = asked
    columns[...] = codes

    pl.semaphore_wait(barrier, OWNERS - 1)
    for step in range(1, OWNERS):
        row = pl.ds(step, 1)
        copy(wanted.at[row], requests.at[row], step, -1, 0, step // PER).start()
    requests[pl.ds(0, 1), :] = asked[0:1, :]
    for load in loads[1:]:
        load.wait()

    def turn_points(g):
        rows = pl.ds(g * GF, GF)
        stacked = jnp.concatenate([r[rows, :] for r in (query_ref, key_ref, value_ref, grad_ref)], axis=0)
        points_in[g][...] = jnp.transpose(stacked)

    chunk_row = iota((CHUNK, 128), 0)
    chunk_lane = iota((CHUNK, 128), 1)
    weight = jnp.where(chunk_lane == chunk_row % SLOT, 16.0, 0.0) + jnp.where(chunk_lane == chunk_row % SLOT + SLOT, 1.0, 0.0)
    spread = onehot(iota((CHUNK, PER), 1) == iota((CHUNK, PER), 0) // SLOT)
    ones = jnp.ones((128, POINTS), BF16)
    number = (iota((CHUNK, POINTS), 1) + 1).astype(F32)

    def send(src, dst, k, sign, number):
        for step in range(max(1, k * PER), (k + 1) * PER):
            rows = pl.ds(step * SLOT, SLOT)
            copy(src.at[rows], dst.at[rows], step, sign, number, CHUNKS - 1 + number).start()
        if k == 0:
            dst[pl.ds(0, SLOT), :] = src[pl.ds(0, SLOT), :]

    turn_points(0)
    for k in range(CHUNKS):
        rows = pl.ds(k * CHUNK, CHUNK)
        wait_all(requests.at[pl.ds(max(1, k * PER), PER - (k == 0))], recv_sem.at[k])
        asks = dot(spread, requests[pl.ds(k * PER, PER), :].astype(BF16)) * weight
        picked = onehot(dot(asks.astype(BF16), ones) == number)
        pick[rows, :] = picked
        out0[rows, :] = dot(picked, points0[...]).astype(BF16)
        send(out0, in0, k, 1, 1)
    turn_points(1)
    for k in range(CHUNKS):
        rows = pl.ds(k * CHUNK, CHUNK)
        out1[rows, :] = dot(pick[rows, :], points1[...]).astype(BF16)
        send(out1, in1, k, 1, 2)

    @pl.loop(0, CHUNKS)
    def _(k):
        rows = pl.ds(pl.multiple_of(k * CHUNK, CHUNK), CHUNK)
        pick_t[:, rows] = jnp.transpose(pick[rows, :])

    codes_t = jnp.transpose(columns[...]).astype(jnp.int32)
    for n in range(BUCKETS):
        t, b = n // 4, n % 4
        code = columns[:, n : n + 1].astype(jnp.int32)
        gather[pl.ds(n * BUCKET, BUCKET), :] = onehot(iota((BUCKET, TROWS), 1) == code)
        gather_t[t, :, pl.ds(b * BUCKET, BUCKET)] = onehot(iota((TROWS, BUCKET), 0) == codes_t[n : n + 1, :])

    packed_row = iota((TABLES * TCHUNK, CHUNK), 0)
    within = packed_row % TCHUNK
    split = onehot(
        iota((TABLES * TCHUNK, CHUNK), 1) == SLOT * (within // CAP) + CAP * (packed_row // TCHUNK) + within % CAP
    )
    packed_lane = iota((CHUNK, TABLES * TCHUNK), 1)
    within = packed_lane % TCHUNK
    merge = onehot(
        iota((CHUNK, TABLES * TCHUNK), 0) == SLOT * (within // CAP) + CAP * (packed_lane // TCHUNK) + within % CAP
    )

    scale = HEAD_DIM**-0.5
    log2e = 1.4426950408889634
    feature = iota((BUCKET, GF), 1) // HEAD_DIM
    heads = [onehot(feature == h) for h in range(GH)]

    def attend(g, n):
        span = pl.ds(pl.multiple_of(n * BUCKET, BUCKET), BUCKET)
        tile = tiles[span, :]
        full = tile.astype(F32)
        turned = jnp.transpose(full)
        q_low, k_low, v_low, g_low = (tile[:, i * GF : (i + 1) * GF] for i in range(4))
        k_full = full[:, GF : 2 * GF]
        q_t, k_t, v_t, g_t = (turned[i * GF : (i + 1) * GF] for i in range(4))

        def spread_t(part):
            blocks = []
            for h in range(GH):
                pieces = [part[h * HEAD_DIM : (h + 1) * HEAD_DIM]]
                if h > 0:
                    pieces = [jnp.zeros((h * HEAD_DIM, BUCKET), F32)] + pieces
                if h < GH - 1:
                    pieces = pieces + [jnp.zeros(((GH - 1 - h) * HEAD_DIM, BUCKET), F32)]
                blocks.append(jnp.concatenate(pieces, axis=0))
            return jnp.concatenate(blocks, axis=1).astype(BF16)

        def spread_rows(part):
            return jnp.concatenate([part * head for head in heads], axis=0)

        squares = k_full * k_full
        dots = dot(k_low, spread_t(q_t))
        dprob = dot(v_low, spread_t(g_t))
        yield
        logits = jnp.concatenate(
            [
                dots[:, h * BUCKET : (h + 1) * BUCKET]
                - 0.5 * jnp.sum(jnp.where(feature == h, squares, 0.0), axis=1, keepdims=True)
                for h in range(GH)
            ],
            axis=1,
        )
        top = jnp.max(logits, axis=0, keepdims=True)
        expons = jnp.exp2((logits - top) * (scale * log2e))
        probs = expons * (1.0 / jnp.sum(expons, axis=0, keepdims=True))
        probs_low = probs.astype(BF16)
        yield

        def paired(left, right):
            left = left.astype(BF16)
            parts = []
            for u in range(GH // 2):
                both = dot(left[2 * HEAD_DIM * u : 2 * HEAD_DIM * (u + 1)], right[:, 2 * BUCKET * u : 2 * BUCKET * (u + 1)])
                parts += [both[:HEAD_DIM, :BUCKET], both[HEAD_DIM:, BUCKET:]]
            return parts

        delta = jnp.concatenate(
            [
                jnp.sum(part * g_t[h * HEAD_DIM : (h + 1) * HEAD_DIM], axis=0, keepdims=True)
                for h, part in enumerate(paired(v_t, probs_low))
            ],
            axis=1,
        )
        value_part = dot(probs_low, spread_rows(g_low)).astype(BF16)
        yield
        dscore = scale * probs * (dprob - delta)
        dscore_low = dscore.astype(BF16)
        sums = jnp.zeros((BUCKET, GF), F32)
        for h in range(GH):
            total = jnp.sum(dscore[:, h * BUCKET : (h + 1) * BUCKET], axis=1, keepdims=True)
            sums = jnp.where(feature == h, total, sums)
        yield
        query_part = jnp.transpose(jnp.concatenate(paired(k_t, dscore_low), axis=0)).astype(BF16)
        key_part = (dot(dscore_low, spread_rows(q_low)) - sums * k_full).astype(BF16)
        if g == 0:
            grads0[span, :] = jnp.concatenate([query_part, key_part, value_part[:, :64]], axis=1)
            grads1[span, 288:320] = value_part[:, 64:]
        else:
            grads1[span, 0:288] = jnp.concatenate([query_part, key_part, value_part], axis=1)

    grads1[:, 256:384] = jnp.zeros((BUCKETS * BUCKET, 128), BF16)
    for g in range(GROUPS):
        wait_all(ins[g].at[pl.ds(SLOT, ROWS - SLOT)], recv_sem.at[CHUNKS + g])
        for k in range(CHUNKS):
            part = dot(split, ins[g][pl.ds(k * CHUNK, CHUNK), :]).astype(BF16)
            for t in range(TABLES):
                rows_of[t, pl.ds(k * TCHUNK, TCHUNK), :] = part[t * TCHUNK : (t + 1) * TCHUNK]
        for t in range(TABLES):
            rows = pl.ds(t * POINTS, POINTS)
            tiles[rows, :] = dot(gather[rows, :], rows_of[t]).astype(BF16)

        @pl.loop(0, BUCKETS // TOGETHER)
        def _(n, g=g):
            running = [attend(g, n * TOGETHER + i) for i in range(TOGETHER)]
            while running:
                running = [r for r in running if next(r, 0) is None]

        for t in range(TABLES):
            slots[g][t] = dot(gather_t[t], grads[g][pl.ds(t * POINTS, POINTS), :]).astype(BF16)
        for k in range(CHUNKS):
            part = jnp.concatenate([slots[g][t, pl.ds(k * TCHUNK, TCHUNK), :] for t in range(TABLES)], axis=0)
            backs[g][pl.ds(k * CHUNK, CHUNK), :] = dot(merge, part).astype(BF16)
            send(backs[g], homes[g], k, -1, 3 + g)

    for g in range(GROUPS):
        wait_all(homes[g].at[pl.ds(SLOT, ROWS - SLOT)], recv_sem.at[CHUNKS + 2 + g])
        result = jnp.transpose(dot(pick_t[...], homes[g][...])).astype(BF16)
        mine = pl.ds(g * GF, GF)
        query_out[mine, :] = result[0:GF]
        key_out[mine, :] = result[GF : 2 * GF]
        if g == 0:
            value_out[pl.ds(0, 64), :] = result[192:256]
        else:
            value_out[mine, :] = result[192:288]
            value_out[pl.ds(64, 32), :] = result[288:320]

    wait_all(wanted.at[pl.ds(1, OWNERS - 1)], send_sem.at[0])
    for g in range(GROUPS):
        wait_all(outs[g].at[pl.ds(SLOT, ROWS - SLOT)], send_sem.at[1 + g])
        wait_all(backs[g].at[pl.ds(SLOT, ROWS - SLOT)], send_sem.at[3 + g])


def on_device(query, key_rows, value, out_grad, members):
    shape = jax.ShapeDtypeStruct(query.shape, BF16)
    vmem = pl.BlockSpec(memory_space=pltpu.VMEM)
    return pl.pallas_call(
        kernel,
        name="hept_backward",
        out_shape=(shape, shape, shape),
        in_specs=[pl.BlockSpec(memory_space=pl.ANY)] * 5,
        out_specs=(vmem,) * 3,
        scratch_shapes=[
            *[pltpu.VMEM(query.shape, BF16)] * 4,
            pltpu.VMEM(members.shape, jnp.int32),
            *[pltpu.VMEM((128, 128), F32)] * 3,
            *[pltpu.VMEM((POINTS, WIDE), BF16)] * 2,
            pltpu.VMEM((ROWS, POINTS), BF16),
            pltpu.VMEM((POINTS, ROWS), BF16),
            pltpu.VMEM((BUCKETS * BUCKET, TROWS), BF16),
            pltpu.VMEM((TABLES, TROWS, POINTS), BF16),
            *[pltpu.VMEM((ROWS, WIDE), BF16)] * 4,
            pltpu.VMEM((TABLES, TROWS, WIDE), BF16),
            pltpu.VMEM((BUCKETS * BUCKET, WIDE), BF16),
            *[pltpu.VMEM((BUCKETS * BUCKET, width), BF16) for width in BACK],
            *[pltpu.VMEM((TABLES, TROWS, width), BF16) for width in BACK],
            *[pltpu.VMEM((ROWS, width), BF16) for width in BACK],
            *[pltpu.VMEM((ROWS, width), BF16) for width in BACK],
            pltpu.SemaphoreType.DMA((5,)),
            pltpu.SemaphoreType.DMA((5,)),
            pltpu.SemaphoreType.DMA((CHUNKS + 4,)),
        ],
        compiler_params=pltpu.CompilerParams(
            collective_id=0, has_side_effects=True, vmem_limit_bytes=56 * 1024 * 1024
        ),
    )(query, key_rows, value, out_grad, members)


def solution(mesh):
    in_specs = (
        P(None, ("phi", "eta")),
        P(None, ("phi", "eta")),
        P(None, ("phi", "eta")),
        P(None, ("phi", "eta")),
        P(None, ("phi", "eta"), None),
    )
    out_specs = (P(None, ("phi", "eta")), P(None, ("phi", "eta")), P(None, ("phi", "eta")))
    return jax.shard_map(
        on_device, mesh=mesh, in_specs=in_specs, out_specs=out_specs, check_vma=False
    )
```

```python
import functools

import jax
import jax.numpy as jnp
from jax import lax
from jax.experimental import pallas as pl
from jax.experimental.pallas import tpu as pltpu
from jax.sharding import PartitionSpec as P

HEADS = 8
HEAD_DIM = 24
TABLES = 3
BUCKET = 128
BUCKETS = 12
POINTS = 512
OWNERS = 128
CAP = 5
SLOT = 16
ROWS = OWNERS * SLOT
TROWS = OWNERS * CAP
GROUPS = 2
GH = HEADS // GROUPS
GF = GH * HEAD_DIM
WIDE = 4 * GF
FEAT = HEADS * HEAD_DIM
BACK = (256, 384)
CHUNK = 256
CHUNKS = ROWS // CHUNK
PER = CHUNK // SLOT
TCHUNK = PER * CAP
TOGETHER = 2
PARTS = 4


def hops(shift):
    return sum((0, 1, 2, 1)[shift // n % 4] for n in (32, 4, 1))


ORDER = [0] + sorted(((j * 37) % OWNERS for j in range(1, OWNERS)), key=hops)
MESH = pl.DeviceIdType.MESH
F32 = jnp.float32
BF16 = jnp.bfloat16


def dot(a, b):
    return jnp.dot(a, b, preferred_element_type=F32)


def iota(shape, dim):
    return lax.broadcasted_iota(jnp.int32, shape, dim)


def place():
    phi, eta = lax.axis_index("phi"), lax.axis_index("eta")
    return phi // 2, phi % 2, eta // 4, eta % 4


def torus():
    x, core, z, y = place()
    xs = [((x + a) % 4) * 2 for a in range(4)]
    cores = [core, 1 - core]
    zs = [((z + a) % 4) * 4 for a in range(4)]
    ys = [(y + a) % 4 for a in range(4)]

    def peer(step, sign):
        shift = ORDER[step]
        a, c, d = (sign * (shift // n) % 4 for n in (32, 4, 1))
        return (xs[a] + cores[shift // 16 % 2], zs[c] + ys[d])

    return peer


def onehot(mask):
    return jnp.where(mask, 1.0, 0.0).astype(BF16)


def kernel(
    query_any, key_any, value_any, grad_any, members_any,
    result_ref,
    query_ref, key_ref, value_ref, grad_ref, members_ref,
    columns, wanted, requests, points0, points1, pick, pick_t, gather, gather_t,
    out0, out1, in0, in1, rows_of, tiles, grads0, grads1, slots0, slots1, back0, back1, home0, home1,
    load_sem, send_sem, recv_sem,
):
    points_in, outs, ins = (points0, points1), (out0, out1), (in0, in1)
    grads, slots, backs, homes = (grads0, grads1), (slots0, slots1), (back0, back1), (home0, home1)
    peer = torus()

    def copy(src, dst, step, sign, sent, received):
        return pltpu.make_async_remote_copy(
            src_ref=src, dst_ref=dst, send_sem=send_sem.at[sent], recv_sem=recv_sem.at[received],
            device_id=peer(step, sign), device_id_type=MESH,
        )

    def wait_all(ref, sem):
        pltpu.make_async_copy(ref, ref, sem).wait()

    barrier = pltpu.get_barrier_semaphore()
    loads = [
        pltpu.make_async_copy(src, dst, load_sem.at[i])
        for i, (src, dst) in enumerate(
            [
                (members_any, members_ref),
                (query_any, query_ref),
                (key_any, key_ref),
                (value_any, value_ref),
                (grad_any, grad_ref),
            ]
        )
    ]
    for load in loads:
        load.start()
    for step in range(1, OWNERS):
        pl.semaphore_signal(barrier, inc=1, device_id=peer(step, 1), device_id_type=MESH)
    loads[0].wait()

    x, core, z, y = place()
    ids = jnp.concatenate([members_ref[t] for t in range(TABLES)] + [jnp.zeros((4, 128), jnp.int32)], axis=0)
    source, local = ids >> 9, ids & 511
    shift = (
        (((x - (source >> 5)) & 3) << 5)
        | (((core - (source >> 4)) & 1) << 4)
        | (((z - (source >> 2)) & 3) << 2)
        | ((y - source) & 3)
    )
    step_of = jnp.zeros_like(shift)
    for step in range(1, OWNERS):
        step_of = jnp.where(shift == ORDER[step], step, step_of)
    both = (step_of * 1024 + local).astype(F32)
    columns[...] = jnp.transpose(jnp.concatenate([both, jnp.zeros((112, 128), F32)], axis=0))
    lane = iota((128, 128), 1)
    sub = iota((128, 128), 0)
    below = onehot(lane < sub)
    asked = jnp.zeros((128, 128), F32)
    codes = jnp.zeros((128, 128), F32)
    for t in range(TABLES):
        seen = jnp.zeros((1, 128), F32)
        for b in range(4):
            n = 4 * t + b
            column = columns[:, n : n + 1].astype(jnp.int32)
            step_col, ask = column >> 10, (column & 1023) + 1
            mine = lane == step_col
            mine_f = jnp.where(mine, 1.0, 0.0)
            earlier = dot(below, mine_f.astype(BF16)) + seen
            rank = jnp.sum(jnp.where(mine, earlier, 0.0), axis=1, keepdims=True).astype(jnp.int32)
            seen = seen + jnp.sum(mine_f, axis=0, keepdims=True)
            slot = CAP * t + rank
            asks = jnp.where(lane == slot, ask >> 4, 0) + jnp.where(lane == slot + SLOT, ask & 15, 0)
            mine_t = onehot(sub == step_of[n : n + 1, :])
            asked = asked + dot(mine_t, asks.astype(F32).astype(BF16))
            codes = jnp.where(lane == n, (CAP * step_col + rank).astype(F32), codes)
    wanted[...] = asked
    columns[...] = codes

    pl.semaphore_wait(barrier, OWNERS - 1)

    for step in range(1, OWNERS):
        row = pl.ds(step, 1)
        copy(wanted.at[row], requests.at[row], step, -1, 0, step // PER).start()
    requests[pl.ds(0, 1), :] = asked[0:1, :]
    for load in loads[1:]:
        load.wait()

    def turn_points(g):
        rows = pl.ds(g * GF, GF)
        stacked = jnp.concatenate([r[rows, :] for r in (query_ref, key_ref, value_ref, grad_ref)], axis=0)
        points_in[g][...] = jnp.transpose(stacked)

    chunk_row = iota((CHUNK, 128), 0)
    chunk_lane = iota((CHUNK, 128), 1)
    weight = jnp.where(chunk_lane == chunk_row % SLOT, 16.0, 0.0) + jnp.where(chunk_lane == chunk_row % SLOT + SLOT, 1.0, 0.0)
    spread = onehot(iota((CHUNK, PER), 1) == iota((CHUNK, PER), 0) // SLOT)
    ones = jnp.ones((128, POINTS), BF16)
    number = (iota((CHUNK, POINTS), 1) + 1).astype(F32)

    def send(src, dst, k, sign, number, received):
        for step in range(max(1, k * PER), (k + 1) * PER):
            rows = pl.ds(step * SLOT, SLOT)
            copy(src.at[rows], dst.at[rows], step, sign, number, received).start()
        if k == 0:
            dst[pl.ds(0, SLOT), :] = src[pl.ds(0, SLOT), :]

    turn_points(0)
    for k in range(CHUNKS):
        rows = pl.ds(k * CHUNK, CHUNK)
        wait_all(requests.at[pl.ds(max(1, k * PER), PER - (k == 0))], recv_sem.at[k])
        asks = dot(spread, requests[pl.ds(k * PER, PER), :].astype(BF16)) * weight
        picked = onehot(dot(asks.astype(BF16), ones) == number)
        pick[rows, :] = picked
        out0[rows, :] = dot(picked, points0[...]).astype(BF16)
        send(out0, in0, k, 1, 1, CHUNKS)
    turn_points(1)
    for k in range(CHUNKS):
        rows = pl.ds(k * CHUNK, CHUNK)
        out1[rows, :] = dot(pick[rows, :], points1[...]).astype(BF16)
        send(out1, in1, k, 1, 2, CHUNKS + 1)

    @pl.loop(0, CHUNKS)
    def _(k):
        rows = pl.ds(pl.multiple_of(k * CHUNK, CHUNK), CHUNK)
        pick_t[:, rows] = jnp.transpose(pick[rows, :])

    codes_t = jnp.transpose(columns[...]).astype(jnp.int32)
    for n in range(BUCKETS):
        t, b = n // 4, n % 4
        code = columns[:, n : n + 1].astype(jnp.int32)
        gather[pl.ds(n * BUCKET, BUCKET), :] = onehot(iota((BUCKET, TROWS), 1) == code)
        gather_t[t, :, pl.ds(b * BUCKET, BUCKET)] = onehot(iota((TROWS, BUCKET), 0) == codes_t[n : n + 1, :])

    packed_row = iota((TABLES * TCHUNK, CHUNK), 0)
    within = packed_row % TCHUNK
    split = onehot(
        iota((TABLES * TCHUNK, CHUNK), 1) == SLOT * (within // CAP) + CAP * (packed_row // TCHUNK) + within % CAP
    )
    packed_lane = iota((CHUNK, TABLES * TCHUNK), 1)
    within = packed_lane % TCHUNK
    merge = onehot(
        iota((CHUNK, TABLES * TCHUNK), 0) == SLOT * (within // CAP) + CAP * (packed_lane // TCHUNK) + within % CAP
    )

    scale = HEAD_DIM**-0.5
    log2e = 1.4426950408889634
    feature = iota((BUCKET, GF), 1) // HEAD_DIM
    heads = [onehot(feature == h) for h in range(GH)]
    term_heads = onehot(iota((24, GH * BUCKET), 0) % 8 == iota((24, GH * BUCKET), 1) // BUCKET)

    def attend(g, n):
        span = pl.ds(pl.multiple_of(n * BUCKET, BUCKET), BUCKET)
        tile = tiles[span, :]
        full = tile.astype(F32)
        turned = jnp.transpose(full)
        q_low, k_low, v_low, g_low = (tile[:, i * GF : (i + 1) * GF] for i in range(4))
        k_full = full[:, GF : 2 * GF]
        q_t, k_t, v_t, g_t = (turned[i * GF : (i + 1) * GF] for i in range(4))

        def spread_t(part):
            blocks = []
            for h in range(GH):
                pieces = [part[h * HEAD_DIM : (h + 1) * HEAD_DIM]]
                if h > 0:
                    pieces = [jnp.zeros((h * HEAD_DIM, BUCKET), F32)] + pieces
                if h < GH - 1:
                    pieces = pieces + [jnp.zeros(((GH - 1 - h) * HEAD_DIM, BUCKET), F32)]
                blocks.append(jnp.concatenate(pieces, axis=0))
            return jnp.concatenate(blocks, axis=1).astype(BF16)

        def spread_rows(part):
            return jnp.concatenate([part * head for head in heads], axis=0)

        norms = jnp.concatenate(
            [
                -0.5 * jnp.sum(k_t[h * HEAD_DIM : (h + 1) * HEAD_DIM] ** 2, axis=0, keepdims=True)
                for h in range(GH)
            ]
            + [jnp.zeros((8 - GH, BUCKET), F32)],
            axis=0,
        )
        terms = []
        for _ in range(3):
            terms.append(norms.astype(BF16).astype(F32))
            norms = norms - terms[-1]
        terms = jnp.transpose(jnp.concatenate(terms, axis=0)).astype(BF16)
        logits = dot(jnp.concatenate([k_low, terms], axis=1), jnp.concatenate([spread_t(q_t), term_heads], axis=0))
        dprob = dot(v_low, spread_t(g_t))
        yield
        top = jnp.max(logits, axis=0, keepdims=True)
        expons = jnp.exp2((logits - top) * (scale * log2e))
        probs = expons * (1.0 / jnp.sum(expons, axis=0, keepdims=True))
        probs_low = probs.astype(BF16)
        yield

        def paired(left, right):
            left = left.astype(BF16)
            parts = []
            for u in range(GH // 2):
                both = dot(left[2 * HEAD_DIM * u : 2 * HEAD_DIM * (u + 1)], right[:, 2 * BUCKET * u : 2 * BUCKET * (u + 1)])
                parts += [both[:HEAD_DIM, :BUCKET], both[HEAD_DIM:, BUCKET:]]
            return parts

        delta = jnp.concatenate(
            [
                jnp.sum(part * g_t[h * HEAD_DIM : (h + 1) * HEAD_DIM], axis=0, keepdims=True)
                for h, part in enumerate(paired(v_t, probs_low))
            ],
            axis=1,
        )
        value_part = dot(probs_low, spread_rows(g_low)).astype(BF16)
        yield
        dscore = scale * probs * (dprob - delta)
        dscore_low = dscore.astype(BF16)
        sums = jnp.zeros((BUCKET, GF), F32)
        for h in range(GH):
            total = jnp.sum(dscore[:, h * BUCKET : (h + 1) * BUCKET], axis=1, keepdims=True)
            sums = jnp.where(feature == h, total, sums)
        yield
        query_part = jnp.transpose(jnp.concatenate(paired(k_t, dscore_low), axis=0)).astype(BF16)
        key_part = (dot(dscore_low, spread_rows(q_low)) - sums * k_full).astype(BF16)
        if g == 0:
            grads0[span, :] = jnp.concatenate([query_part, key_part, value_part[:, :64]], axis=1)
            grads1[span, 288:320] = value_part[:, 64:]
        else:
            grads1[span, 0:288] = jnp.concatenate([query_part, key_part, value_part], axis=1)

    grads1[:, 256:384] = jnp.zeros((BUCKETS * BUCKET, 128), BF16)
    for g in range(GROUPS):
        wait_all(ins[g].at[pl.ds(SLOT, ROWS - SLOT)], recv_sem.at[CHUNKS + g])
        for k in range(CHUNKS):
            part = dot(split, ins[g][pl.ds(k * CHUNK, CHUNK), :]).astype(BF16)
            for t in range(TABLES):
                rows_of[t, pl.ds(k * TCHUNK, TCHUNK), :] = part[t * TCHUNK : (t + 1) * TCHUNK]
        for t in range(TABLES):
            rows = pl.ds(t * POINTS, POINTS)
            tiles[rows, :] = dot(gather[rows, :], rows_of[t]).astype(BF16)

        @pl.loop(0, BUCKETS // TOGETHER)
        def _(n, g=g):
            running = [attend(g, n * TOGETHER + i) for i in range(TOGETHER)]
            while running:
                running = [r for r in running if next(r, 0) is None]

        for t in range(TABLES):
            slots[g][t] = dot(gather_t[t], grads[g][pl.ds(t * POINTS, POINTS), :]).astype(BF16)
        for k in range(CHUNKS):
            part = jnp.concatenate([slots[g][t, pl.ds(k * TCHUNK, TCHUNK), :] for t in range(TABLES)], axis=0)
            backs[g][pl.ds(k * CHUNK, CHUNK), :] = dot(merge, part).astype(BF16)
            send(backs[g], homes[g], k, -1, 3 + g, CHUNKS + GROUPS + g * PARTS + k // (CHUNKS // PARTS))

    for g in range(GROUPS):
        total = jnp.zeros((POINTS, BACK[g]), F32)
        for p in range(PARTS):
            part = ROWS // PARTS
            wait_all(homes[g].at[pl.ds(max(SLOT, p * part), part - SLOT * (p == 0))], recv_sem.at[CHUNKS + GROUPS + g * PARTS + p])
            total = total + dot(pick_t[:, p * part : (p + 1) * part], homes[g][pl.ds(p * part, part), :])
        result = jnp.transpose(total).astype(BF16)
        for i in range(2):
            result_ref[pl.ds(i * FEAT + g * GF, GF), :] = result[i * GF : (i + 1) * GF]
        if g == 0:
            result_ref[pl.ds(2 * FEAT, 64), :] = result[192:256]
        else:
            result_ref[pl.ds(2 * FEAT + GF, GF), :] = result[192:288]
            result_ref[pl.ds(2 * FEAT + 64, 32), :] = result[288:320]

    wait_all(wanted.at[pl.ds(1, OWNERS - 1)], send_sem.at[0])
    for g in range(GROUPS):
        wait_all(outs[g].at[pl.ds(SLOT, ROWS - SLOT)], send_sem.at[1 + g])
        wait_all(backs[g].at[pl.ds(SLOT, ROWS - SLOT)], send_sem.at[3 + g])


def divide(result_ref, query_out, key_out, value_out):
    for i, out in enumerate((query_out, key_out, value_out)):
        out[...] = result_ref[pl.ds(i * FEAT, FEAT), :]


def on_device(query, key_rows, value, out_grad, members):
    shape = jax.ShapeDtypeStruct(query.shape, BF16)
    vmem = pl.BlockSpec(memory_space=pltpu.VMEM)
    result = pl.pallas_call(
        kernel,
        name="hept_backward",
        out_shape=jax.ShapeDtypeStruct((3 * FEAT, POINTS), BF16),
        in_specs=[pl.BlockSpec(memory_space=pl.ANY)] * 5,
        out_specs=vmem,
        scratch_shapes=[
            *[pltpu.VMEM(query.shape, BF16)] * 4,
            pltpu.VMEM(members.shape, jnp.int32),
            *[pltpu.VMEM((128, 128), F32)] * 3,
            *[pltpu.VMEM((POINTS, WIDE), BF16)] * 2,
            pltpu.VMEM((ROWS, POINTS), BF16),
            pltpu.VMEM((POINTS, ROWS), BF16),
            pltpu.VMEM((BUCKETS * BUCKET, TROWS), BF16),
            pltpu.VMEM((TABLES, TROWS, POINTS), BF16),
            *[pltpu.VMEM((ROWS, WIDE), BF16)] * 4,
            pltpu.VMEM((TABLES, TROWS, WIDE), BF16),
            pltpu.VMEM((BUCKETS * BUCKET, WIDE), BF16),
            *[pltpu.VMEM((BUCKETS * BUCKET, width), BF16) for width in BACK],
            *[pltpu.VMEM((TABLES, TROWS, width), BF16) for width in BACK],
            *[pltpu.VMEM((ROWS, width), BF16) for width in BACK],
            *[pltpu.VMEM((ROWS, width), BF16) for width in BACK],
            pltpu.SemaphoreType.DMA((5,)),
            pltpu.SemaphoreType.DMA((5,)),
            pltpu.SemaphoreType.DMA((CHUNKS + GROUPS + GROUPS * PARTS,)),
        ],
        compiler_params=pltpu.CompilerParams(
            collective_id=0, has_side_effects=True, vmem_limit_bytes=56 * 1024 * 1024
        ),
    )(query, key_rows, value, out_grad, members)
    return pl.pallas_call(
        divide, name="divide", out_shape=(shape,) * 3, in_specs=[vmem], out_specs=(vmem,) * 3
    )(result)


def solution(mesh):
    in_specs = (
        P(None, ("phi", "eta")),
        P(None, ("phi", "eta")),
        P(None, ("phi", "eta")),
        P(None, ("phi", "eta")),
        P(None, ("phi", "eta"), None),
    )
    out_specs = (P(None, ("phi", "eta")), P(None, ("phi", "eta")), P(None, ("phi", "eta")))
    return jax.shard_map(
        on_device, mesh=mesh, in_specs=in_specs, out_specs=out_specs, check_vma=False
    )
```

```python
import functools

import jax
import jax.numpy as jnp
from jax import lax
from jax.experimental import pallas as pl
from jax.experimental.pallas import tpu as pltpu
from jax.sharding import PartitionSpec as P

HEADS = 8
HEAD_DIM = 24
TABLES = 3
BUCKET = 128
BUCKETS = 12
POINTS = 512
OWNERS = 128
CAP = 5
SLOT = 16
ROWS = OWNERS * SLOT
TROWS = OWNERS * CAP
GROUPS = 2
GH = HEADS // GROUPS
GF = GH * HEAD_DIM
WIDE = 4 * GF
FEAT = HEADS * HEAD_DIM
GRADS = (256, 384)
BACK = 256
TAIL = SLOT // 2
CHUNK = 256
CHUNKS = ROWS // CHUNK
PER = CHUNK // SLOT
TCHUNK = PER * CAP
TOGETHER = 2
PARTS = 4


def hops(shift):
    return sum((0, 1, 2, 1)[shift // n % 4] for n in (32, 4, 1))


ORDER = [0] + sorted(((j * 37) % OWNERS for j in range(1, OWNERS)), key=hops)
MESH = pl.DeviceIdType.MESH
F32 = jnp.float32
BF16 = jnp.bfloat16


def dot(a, b):
    return jnp.dot(a, b, preferred_element_type=F32)


def iota(shape, dim):
    return lax.broadcasted_iota(jnp.int32, shape, dim)


def place():
    phi, eta = lax.axis_index("phi"), lax.axis_index("eta")
    return phi // 2, phi % 2, eta // 4, eta % 4


def torus():
    x, core, z, y = place()
    xs = [((x + a) % 4) * 2 for a in range(4)]
    cores = [core, 1 - core]
    zs = [((z + a) % 4) * 4 for a in range(4)]
    ys = [(y + a) % 4 for a in range(4)]

    def peer(step, sign):
        shift = ORDER[step]
        a, c, d = (sign * (shift // n) % 4 for n in (32, 4, 1))
        return (xs[a] + cores[shift // 16 % 2], zs[c] + ys[d])

    return peer


def onehot(mask):
    return jnp.where(mask, 1.0, 0.0).astype(BF16)


def kernel(
    query_any, key_any, value_any, grad_any, members_any,
    result_ref,
    query_ref, key_ref, value_ref, grad_ref, members_ref,
    columns, wanted, requests, points0, points1, pick, pick_t, gather, gather_t,
    out0, out1, in0, in1, rows_of, tiles, grads0, grads1, slots0, slots1, back0, back1, home0, home1, tail_back, tail_home,
    load_sem, send_sem, recv_sem,
):
    points_in, outs, ins = (points0, points1), (out0, out1), (in0, in1)
    grads, slots, backs, homes = (grads0, grads1), (slots0, slots1), (back0, back1), (home0, home1)
    peer = torus()

    def copy(src, dst, step, sign, sent, received):
        return pltpu.make_async_remote_copy(
            src_ref=src, dst_ref=dst, send_sem=send_sem.at[sent], recv_sem=recv_sem.at[received],
            device_id=peer(step, sign), device_id_type=MESH,
        )

    def wait_all(ref, sem):
        pltpu.make_async_copy(ref, ref, sem).wait()

    barrier = pltpu.get_barrier_semaphore()
    loads = [
        pltpu.make_async_copy(src, dst, load_sem.at[i])
        for i, (src, dst) in enumerate(
            [
                (members_any, members_ref),
                (query_any, query_ref),
                (key_any, key_ref),
                (value_any, value_ref),
                (grad_any, grad_ref),
            ]
        )
    ]
    for load in loads:
        load.start()
    for step in range(1, OWNERS):
        pl.semaphore_signal(barrier, inc=1, device_id=peer(step, 1), device_id_type=MESH)
    loads[0].wait()

    x, core, z, y = place()
    ids = jnp.concatenate([members_ref[t] for t in range(TABLES)] + [jnp.zeros((4, 128), jnp.int32)], axis=0)
    source, local = ids >> 9, ids & 511
    shift = (
        (((x - (source >> 5)) & 3) << 5)
        | (((core - (source >> 4)) & 1) << 4)
        | (((z - (source >> 2)) & 3) << 2)
        | ((y - source) & 3)
    )
    step_of = jnp.zeros_like(shift)
    for step in range(1, OWNERS):
        step_of = jnp.where(shift == ORDER[step], step, step_of)
    both = (step_of * 1024 + local).astype(F32)
    columns[...] = jnp.transpose(jnp.concatenate([both, jnp.zeros((112, 128), F32)], axis=0))
    lane = iota((128, 128), 1)
    sub = iota((128, 128), 0)
    below = onehot(lane < sub)
    asked = jnp.zeros((128, 128), F32)
    codes = jnp.zeros((128, 128), F32)
    for t in range(TABLES):
        seen = jnp.zeros((1, 128), F32)
        for b in range(4):
            n = 4 * t + b
            column = columns[:, n : n + 1].astype(jnp.int32)
            step_col, ask = column >> 10, (column & 1023) + 1
            mine = lane == step_col
            mine_f = jnp.where(mine, 1.0, 0.0)
            earlier = dot(below, mine_f.astype(BF16)) + seen
            rank = jnp.sum(jnp.where(mine, earlier, 0.0), axis=1, keepdims=True).astype(jnp.int32)
            seen = seen + jnp.sum(mine_f, axis=0, keepdims=True)
            slot = CAP * t + rank
            asks = jnp.where(lane == slot, ask >> 4, 0) + jnp.where(lane == slot + SLOT, ask & 15, 0)
            mine_t = onehot(sub == step_of[n : n + 1, :])
            asked = asked + dot(mine_t, asks.astype(F32).astype(BF16))
            codes = jnp.where(lane == n, (CAP * step_col + rank).astype(F32), codes)
    wanted[...] = asked
    columns[...] = codes

    pl.semaphore_wait(barrier, OWNERS - 1)

    for step in range(1, OWNERS):
        row = pl.ds(step, 1)
        copy(wanted.at[row], requests.at[row], step, -1, 0, step // PER).start()
    requests[pl.ds(0, 1), :] = asked[0:1, :]
    for load in loads[1:]:
        load.wait()

    def turn_points(g):
        rows = pl.ds(g * GF, GF)
        stacked = jnp.concatenate([r[rows, :] for r in (query_ref, key_ref, value_ref, grad_ref)], axis=0)
        points_in[g][...] = jnp.transpose(stacked)

    chunk_row = iota((CHUNK, 128), 0)
    chunk_lane = iota((CHUNK, 128), 1)
    weight = jnp.where(chunk_lane == chunk_row % SLOT, 16.0, 0.0) + jnp.where(chunk_lane == chunk_row % SLOT + SLOT, 1.0, 0.0)
    spread = onehot(iota((CHUNK, PER), 1) == iota((CHUNK, PER), 0) // SLOT)
    ones = jnp.ones((128, POINTS), BF16)
    number = (iota((CHUNK, POINTS), 1) + 1).astype(F32)

    def send(src, dst, k, sign, number, received):
        for step in range(max(1, k * PER), (k + 1) * PER):
            rows = pl.ds(step * SLOT, SLOT)
            copy(src.at[rows], dst.at[rows], step, sign, number, received).start()
        if k == 0:
            dst[pl.ds(0, SLOT), :] = src[pl.ds(0, SLOT), :]

    turn_points(0)
    for k in range(CHUNKS):
        rows = pl.ds(k * CHUNK, CHUNK)
        wait_all(requests.at[pl.ds(max(1, k * PER), PER - (k == 0))], recv_sem.at[k])
        asks = dot(spread, requests[pl.ds(k * PER, PER), :].astype(BF16)) * weight
        picked = onehot(dot(asks.astype(BF16), ones) == number)
        pick[rows, :] = picked
        out0[rows, :] = dot(picked, points0[...]).astype(BF16)
        send(out0, in0, k, 1, 1, CHUNKS)
    turn_points(1)
    for k in range(CHUNKS):
        rows = pl.ds(k * CHUNK, CHUNK)
        out1[rows, :] = dot(pick[rows, :], points1[...]).astype(BF16)
        send(out1, in1, k, 1, 2, CHUNKS + 1)

    @pl.loop(0, CHUNKS)
    def _(k):
        rows = pl.ds(pl.multiple_of(k * CHUNK, CHUNK), CHUNK)
        pick_t[:, rows] = jnp.transpose(pick[rows, :])

    codes_t = jnp.transpose(columns[...]).astype(jnp.int32)
    for n in range(BUCKETS):
        t, b = n // 4, n % 4
        code = columns[:, n : n + 1].astype(jnp.int32)
        gather[pl.ds(n * BUCKET, BUCKET), :] = onehot(iota((BUCKET, TROWS), 1) == code)
        gather_t[t, :, pl.ds(b * BUCKET, BUCKET)] = onehot(iota((TROWS, BUCKET), 0) == codes_t[n : n + 1, :])

    packed_row = iota((TABLES * TCHUNK, CHUNK), 0)
    within = packed_row % TCHUNK
    split = onehot(
        iota((TABLES * TCHUNK, CHUNK), 1) == SLOT * (within // CAP) + CAP * (packed_row // TCHUNK) + within % CAP
    )
    packed_lane = iota((CHUNK, TABLES * TCHUNK), 1)
    within = packed_lane % TCHUNK
    merge = onehot(
        iota((CHUNK, TABLES * TCHUNK), 0) == SLOT * (within // CAP) + CAP * (packed_lane // TCHUNK) + within % CAP
    )

    tail_row = iota((PER * TAIL, TABLES * TCHUNK), 0)
    within = iota((PER * TAIL, TABLES * TCHUNK), 1) % TCHUNK
    source_row = SLOT * (within // CAP) + CAP * (iota((PER * TAIL, TABLES * TCHUNK), 1) // TCHUNK) + within % CAP
    tail_row = SLOT * (tail_row // TAIL) + tail_row % TAIL
    merge_tail = jnp.concatenate([onehot(tail_row == source_row), onehot(tail_row + TAIL == source_row)], axis=0)

    scale = HEAD_DIM**-0.5
    log2e = 1.4426950408889634
    feature = iota((BUCKET, GF), 1) // HEAD_DIM
    heads = [onehot(feature == h) for h in range(GH)]
    term_heads = onehot(iota((24, GH * BUCKET), 0) % 8 == iota((24, GH * BUCKET), 1) // BUCKET)

    def attend(g, n):
        span = pl.ds(pl.multiple_of(n * BUCKET, BUCKET), BUCKET)
        tile = tiles[span, :]
        full = tile.astype(F32)
        turned = jnp.transpose(full)
        q_low, k_low, v_low, g_low = (tile[:, i * GF : (i + 1) * GF] for i in range(4))
        k_full = full[:, GF : 2 * GF]
        q_t, k_t, v_t, g_t = (turned[i * GF : (i + 1) * GF] for i in range(4))

        def spread_t(part):
            blocks = []
            for h in range(GH):
                pieces = [part[h * HEAD_DIM : (h + 1) * HEAD_DIM]]
                if h > 0:
                    pieces = [jnp.zeros((h * HEAD_DIM, BUCKET), F32)] + pieces
                if h < GH - 1:
                    pieces = pieces + [jnp.zeros(((GH - 1 - h) * HEAD_DIM, BUCKET), F32)]
                blocks.append(jnp.concatenate(pieces, axis=0))
            return jnp.concatenate(blocks, axis=1).astype(BF16)

        def spread_rows(part):
            return jnp.concatenate([part * head for head in heads], axis=0)

        norms = jnp.concatenate(
            [
                -0.5 * jnp.sum(k_t[h * HEAD_DIM : (h + 1) * HEAD_DIM] ** 2, axis=0, keepdims=True)
                for h in range(GH)
            ]
            + [jnp.zeros((8 - GH, BUCKET), F32)],
            axis=0,
        )
        terms = []
        for _ in range(3):
            terms.append(norms.astype(BF16).astype(F32))
            norms = norms - terms[-1]
        terms = jnp.transpose(jnp.concatenate(terms, axis=0)).astype(BF16)
        logits = dot(jnp.concatenate([k_low, terms], axis=1), jnp.concatenate([spread_t(q_t), term_heads], axis=0))
        dprob = dot(v_low, spread_t(g_t))
        yield
        top = jnp.max(logits, axis=0, keepdims=True)
        expons = jnp.exp2((logits - top) * (scale * log2e))
        probs = expons * (1.0 / jnp.sum(expons, axis=0, keepdims=True))
        probs_low = probs.astype(BF16)
        yield

        def paired(left, right):
            left = left.astype(BF16)
            parts = []
            for u in range(GH // 2):
                both = dot(left[2 * HEAD_DIM * u : 2 * HEAD_DIM * (u + 1)], right[:, 2 * BUCKET * u : 2 * BUCKET * (u + 1)])
                parts += [both[:HEAD_DIM, :BUCKET], both[HEAD_DIM:, BUCKET:]]
            return parts

        delta = jnp.concatenate(
            [
                jnp.sum(part * g_t[h * HEAD_DIM : (h + 1) * HEAD_DIM], axis=0, keepdims=True)
                for h, part in enumerate(paired(v_t, probs_low))
            ],
            axis=1,
        )
        value_part = dot(probs_low, spread_rows(g_low)).astype(BF16)
        yield
        dscore = scale * probs * (dprob - delta)
        dscore_low = dscore.astype(BF16)
        sums = jnp.zeros((BUCKET, GF), F32)
        for h in range(GH):
            total = jnp.sum(dscore[:, h * BUCKET : (h + 1) * BUCKET], axis=1, keepdims=True)
            sums = jnp.where(feature == h, total, sums)
        yield
        query_part = jnp.transpose(jnp.concatenate(paired(k_t, dscore_low), axis=0)).astype(BF16)
        key_part = (dot(dscore_low, spread_rows(q_low)) - sums * k_full).astype(BF16)
        grads[g][span, 0:256] = jnp.concatenate([query_part, key_part, value_part[:, :64]], axis=1)
        at = 256 + 32 * (1 - g)
        grads1[span, at : at + 32] = value_part[:, 64:]
        grads1[span, at + 64 : at + 96] = value_part[:, 64:]

    for g in range(GROUPS):
        wait_all(ins[g].at[pl.ds(SLOT, ROWS - SLOT)], recv_sem.at[CHUNKS + g])
        for k in range(CHUNKS):
            part = dot(split, ins[g][pl.ds(k * CHUNK, CHUNK), :]).astype(BF16)
            for t in range(TABLES):
                rows_of[t, pl.ds(k * TCHUNK, TCHUNK), :] = part[t * TCHUNK : (t + 1) * TCHUNK]
        for t in range(TABLES):
            rows = pl.ds(t * POINTS, POINTS)
            tiles[rows, :] = dot(gather[rows, :], rows_of[t]).astype(BF16)

        @pl.loop(0, BUCKETS // TOGETHER)
        def _(n, g=g):
            running = [attend(g, n * TOGETHER + i) for i in range(TOGETHER)]
            while running:
                running = [r for r in running if next(r, 0) is None]

        for t in range(TABLES):
            slots[g][t] = dot(gather_t[t], grads[g][pl.ds(t * POINTS, POINTS), :]).astype(BF16)
        for k in range(CHUNKS):
            part = jnp.concatenate([slots[g][t, pl.ds(k * TCHUNK, TCHUNK), :] for t in range(TABLES)], axis=0)
            backs[g][pl.ds(k * CHUNK, CHUNK), :] = dot(merge, part[:, :BACK]).astype(BF16)
            received = CHUNKS + GROUPS + k // (CHUNKS // PARTS)
            send(backs[g], homes[g], k, -1, 3 + g, received + g * PARTS)
            if g == 1:
                both = dot(merge_tail, part[:, BACK:])
                tail = jnp.where(iota((PER * TAIL, 128), 1) < 64, both[: PER * TAIL], both[PER * TAIL :])
                tail_back[pl.ds(k * PER, PER)] = tail.reshape(PER, TAIL, 128).astype(BF16)
                for step in range(max(1, k * PER), (k + 1) * PER):
                    copy(tail_back.at[step], tail_home.at[step], step, -1, 5, received + 2 * PARTS).start()
                if k == 0:
                    tail_home[0] = tail_back[0]

    part = ROWS // PARTS
    tails = part // 2
    wide = onehot(
        iota((part, tails), 1) == TAIL * (iota((part, tails), 0) // SLOT) + iota((part, tails), 0) % TAIL
    )
    own_half = (iota((part, 128), 0) % SLOT < TAIL) == (iota((part, 128), 1) < 64)
    for g in range(GROUPS):
        total = jnp.zeros((POINTS, GRADS[g]), F32)
        for p in range(PARTS):
            first = SLOT * (p == 0)
            received = CHUNKS + GROUPS + p
            wait_all(homes[g].at[pl.ds(p * part + first, part - first)], recv_sem.at[received + g * PARTS])
            rows = homes[g][pl.ds(p * part, part), :]
            if g == 1:
                owners = part // SLOT
                first = int(p == 0)
                wait_all(tail_home.at[pl.ds(p * owners + first, owners - first)], recv_sem.at[received + 2 * PARTS])
                tail = tail_home[pl.ds(p * owners, owners)].astype(F32).reshape(tails, 128).astype(BF16)
                rows = jnp.concatenate([rows, jnp.where(own_half, dot(wide, tail), 0.0).astype(BF16)], axis=1)
            total = total + dot(pick_t[:, p * part : (p + 1) * part], rows)
        result = jnp.transpose(total)
        for i in range(2):
            result_ref[pl.ds(i * FEAT + g * GF, GF), :] = result[i * GF : (i + 1) * GF].astype(BF16)
        result_ref[pl.ds(2 * FEAT + g * GF, 64), :] = result[192:256].astype(BF16)
    last = (result[256:320] + result[320:384]).astype(BF16)
    result_ref[pl.ds(2 * FEAT + GF + 64, 32), :] = last[:32]
    result_ref[pl.ds(2 * FEAT + 64, 32), :] = last[32:]

    wait_all(wanted.at[pl.ds(1, OWNERS - 1)], send_sem.at[0])
    for g in range(GROUPS):
        wait_all(outs[g].at[pl.ds(SLOT, ROWS - SLOT)], send_sem.at[1 + g])
        wait_all(backs[g].at[pl.ds(SLOT, ROWS - SLOT)], send_sem.at[3 + g])
    wait_all(tail_back.at[pl.ds(1, OWNERS - 1)], send_sem.at[5])


def divide(result_ref, query_out, key_out, value_out):
    for i, out in enumerate((query_out, key_out, value_out)):
        out[...] = result_ref[pl.ds(i * FEAT, FEAT), :]


def on_device(query, key_rows, value, out_grad, members):
    shape = jax.ShapeDtypeStruct(query.shape, BF16)
    vmem = pl.BlockSpec(memory_space=pltpu.VMEM)
    result = pl.pallas_call(
        kernel,
        name="hept_backward",
        out_shape=jax.ShapeDtypeStruct((3 * FEAT, POINTS), BF16),
        in_specs=[pl.BlockSpec(memory_space=pl.ANY)] * 5,
        out_specs=vmem,
        scratch_shapes=[
            *[pltpu.VMEM(query.shape, BF16)] * 4,
            pltpu.VMEM(members.shape, jnp.int32),
            *[pltpu.VMEM((128, 128), F32)] * 3,
            *[pltpu.VMEM((POINTS, WIDE), BF16)] * 2,
            pltpu.VMEM((ROWS, POINTS), BF16),
            pltpu.VMEM((POINTS, ROWS), BF16),
            pltpu.VMEM((BUCKETS * BUCKET, TROWS), BF16),
            pltpu.VMEM((TABLES, TROWS, POINTS), BF16),
            *[pltpu.VMEM((ROWS, WIDE), BF16)] * 4,
            pltpu.VMEM((TABLES, TROWS, WIDE), BF16),
            pltpu.VMEM((BUCKETS * BUCKET, WIDE), BF16),
            *[pltpu.VMEM((BUCKETS * BUCKET, width), BF16) for width in GRADS],
            *[pltpu.VMEM((TABLES, TROWS, width), BF16) for width in GRADS],
            *[pltpu.VMEM((ROWS, BACK), BF16)] * 4,
            *[pltpu.VMEM((OWNERS, TAIL, 128), BF16)] * 2,
            pltpu.SemaphoreType.DMA((5,)),
            pltpu.SemaphoreType.DMA((6,)),
            pltpu.SemaphoreType.DMA((CHUNKS + GROUPS + 3 * PARTS,)),
        ],
        compiler_params=pltpu.CompilerParams(
            collective_id=0, has_side_effects=True, vmem_limit_bytes=56 * 1024 * 1024
        ),
    )(query, key_rows, value, out_grad, members)
    return pl.pallas_call(
        divide, name="divide", out_shape=(shape,) * 3, in_specs=[vmem], out_specs=(vmem,) * 3
    )(result)


def solution(mesh):
    in_specs = (
        P(None, ("phi", "eta")),
        P(None, ("phi", "eta")),
        P(None, ("phi", "eta")),
        P(None, ("phi", "eta")),
        P(None, ("phi", "eta"), None),
    )
    out_specs = (P(None, ("phi", "eta")), P(None, ("phi", "eta")), P(None, ("phi", "eta")))
    return jax.shard_map(
        on_device, mesh=mesh, in_specs=in_specs, out_specs=out_specs, check_vma=False
    )
```

```python
import functools

import jax
import jax.numpy as jnp
from jax import lax
from jax.experimental import pallas as pl
from jax.experimental.pallas import tpu as pltpu
from jax.sharding import PartitionSpec as P

HEADS = 8
HEAD_DIM = 24
TABLES = 3
BUCKET = 128
BUCKETS = 12
POINTS = 512
OWNERS = 128
CAP = 5
SLOT = 16
ROWS = OWNERS * SLOT
TROWS = OWNERS * CAP
GROUPS = 2
GH = HEADS // GROUPS
GF = GH * HEAD_DIM
WIDE = 4 * GF
FEAT = HEADS * HEAD_DIM
GRADS = (256, 384)
BACK = 256
TAIL = SLOT // 2
CHUNK = 256
CHUNKS = ROWS // CHUNK
PER = CHUNK // SLOT
TCHUNK = PER * CAP
TOGETHER = 4
PARTS = 4


def hops(shift):
    return sum((0, 1, 2, 1)[shift // n % 4] for n in (32, 4, 1))


ORDER = [0] + sorted(((j * 37) % OWNERS for j in range(1, OWNERS)), key=hops)
MESH = pl.DeviceIdType.MESH
F32 = jnp.float32
BF16 = jnp.bfloat16


def dot(a, b):
    return jnp.dot(a, b, preferred_element_type=F32)


def iota(shape, dim):
    return lax.broadcasted_iota(jnp.int32, shape, dim)


def place():
    phi, eta = lax.axis_index("phi"), lax.axis_index("eta")
    return phi // 2, phi % 2, eta // 4, eta % 4


def torus():
    x, core, z, y = place()
    xs = [((x + a) % 4) * 2 for a in range(4)]
    cores = [core, 1 - core]
    zs = [((z + a) % 4) * 4 for a in range(4)]
    ys = [(y + a) % 4 for a in range(4)]

    def peer(step, sign):
        shift = ORDER[step]
        a, c, d = (sign * (shift // n) % 4 for n in (32, 4, 1))
        return (xs[a] + cores[shift // 16 % 2], zs[c] + ys[d])

    return peer


def onehot(mask):
    return jnp.where(mask, 1.0, 0.0).astype(BF16)


def kernel(
    query_any, key_any, value_any, grad_any, members_any,
    result_ref,
    query_ref, key_ref, value_ref, grad_ref, members_ref,
    columns, wanted, requests, points0, points1, pick, pick_t, gather, gather_t,
    out0, out1, in0, in1, rows_of, tiles, grads0, grads1, slots0, slots1, back0, back1, home0, home1, tail_back, tail_home,
    load_sem, send_sem, recv_sem,
):
    points_in, outs, ins = (points0, points1), (out0, out1), (in0, in1)
    grads, slots, backs, homes = (grads0, grads1), (slots0, slots1), (back0, back1), (home0, home1)
    peer = torus()

    def copy(src, dst, step, sign, sent, received):
        return pltpu.make_async_remote_copy(
            src_ref=src, dst_ref=dst, send_sem=send_sem.at[sent], recv_sem=recv_sem.at[received],
            device_id=peer(step, sign), device_id_type=MESH,
        )

    def wait_all(ref, sem):
        pltpu.make_async_copy(ref, ref, sem).wait()

    barrier = pltpu.get_barrier_semaphore()
    loads = [
        pltpu.make_async_copy(src, dst, load_sem.at[i])
        for i, (src, dst) in enumerate(
            [
                (members_any, members_ref),
                (query_any, query_ref),
                (key_any, key_ref),
                (value_any, value_ref),
                (grad_any, grad_ref),
            ]
        )
    ]
    for load in loads:
        load.start()
    for step in range(1, OWNERS):
        pl.semaphore_signal(barrier, inc=1, device_id=peer(step, 1), device_id_type=MESH)
    loads[0].wait()

    x, core, z, y = place()
    ids = jnp.concatenate([members_ref[t] for t in range(TABLES)] + [jnp.zeros((4, 128), jnp.int32)], axis=0)
    source, local = ids >> 9, ids & 511
    shift = (
        (((x - (source >> 5)) & 3) << 5)
        | (((core - (source >> 4)) & 1) << 4)
        | (((z - (source >> 2)) & 3) << 2)
        | ((y - source) & 3)
    )
    step_of = jnp.zeros_like(shift)
    for step in range(1, OWNERS):
        step_of = jnp.where(shift == ORDER[step], step, step_of)
    both = (step_of * 1024 + local).astype(F32)
    columns[...] = jnp.transpose(jnp.concatenate([both, jnp.zeros((112, 128), F32)], axis=0))
    lane = iota((128, 128), 1)
    sub = iota((128, 128), 0)
    below = onehot(lane < sub)
    asked = jnp.zeros((128, 128), F32)
    codes = jnp.zeros((128, 128), F32)
    for t in range(TABLES):
        seen = jnp.zeros((1, 128), F32)
        for b in range(4):
            n = 4 * t + b
            column = columns[:, n : n + 1].astype(jnp.int32)
            step_col, ask = column >> 10, (column & 1023) + 1
            mine = lane == step_col
            mine_f = jnp.where(mine, 1.0, 0.0)
            earlier = dot(below, mine_f.astype(BF16)) + seen
            rank = jnp.sum(jnp.where(mine, earlier, 0.0), axis=1, keepdims=True).astype(jnp.int32)
            seen = seen + jnp.sum(mine_f, axis=0, keepdims=True)
            slot = CAP * t + rank
            asks = jnp.where(lane == slot, ask >> 4, 0) + jnp.where(lane == slot + SLOT, ask & 15, 0)
            mine_t = onehot(sub == step_of[n : n + 1, :])
            asked = asked + dot(mine_t, asks.astype(F32).astype(BF16))
            codes = jnp.where(lane == n, (CAP * step_col + rank).astype(F32), codes)
    wanted[...] = asked
    columns[...] = codes

    pl.semaphore_wait(barrier, OWNERS - 1)

    for step in range(1, OWNERS):
        row = pl.ds(step, 1)
        copy(wanted.at[row], requests.at[row], step, -1, 0, step // PER).start()
    requests[pl.ds(0, 1), :] = asked[0:1, :]
    for load in loads[1:]:
        load.wait()

    def turn_points(g):
        rows = pl.ds(g * GF, GF)
        stacked = jnp.concatenate([r[rows, :] for r in (query_ref, key_ref, value_ref, grad_ref)], axis=0)
        points_in[g][...] = jnp.transpose(stacked)

    chunk_row = iota((CHUNK, 128), 0)
    chunk_lane = iota((CHUNK, 128), 1)
    weight = jnp.where(chunk_lane == chunk_row % SLOT, 16.0, 0.0) + jnp.where(chunk_lane == chunk_row % SLOT + SLOT, 1.0, 0.0)
    spread = onehot(iota((CHUNK, PER), 1) == iota((CHUNK, PER), 0) // SLOT)
    ones = jnp.ones((128, POINTS), BF16)
    number = (iota((CHUNK, POINTS), 1) + 1).astype(F32)

    def send(src, dst, k, sign, number, received):
        for step in range(max(1, k * PER), (k + 1) * PER):
            rows = pl.ds(step * SLOT, SLOT)
            copy(src.at[rows], dst.at[rows], step, sign, number, received).start()
        if k == 0:
            dst[pl.ds(0, SLOT), :] = src[pl.ds(0, SLOT), :]

    turn_points(0)
    for k in range(CHUNKS):
        rows = pl.ds(k * CHUNK, CHUNK)
        wait_all(requests.at[pl.ds(max(1, k * PER), PER - (k == 0))], recv_sem.at[k])
        asks = dot(spread, requests[pl.ds(k * PER, PER), :].astype(BF16)) * weight
        picked = onehot(dot(asks.astype(BF16), ones) == number)
        pick[rows, :] = picked
        out0[rows, :] = dot(picked, points0[...]).astype(BF16)
        send(out0, in0, k, 1, 1, CHUNKS)
    turn_points(1)
    for k in range(CHUNKS):
        rows = pl.ds(k * CHUNK, CHUNK)
        out1[rows, :] = dot(pick[rows, :], points1[...]).astype(BF16)
        send(out1, in1, k, 1, 2, CHUNKS + 1)

    @pl.loop(0, CHUNKS)
    def _(k):
        rows = pl.ds(pl.multiple_of(k * CHUNK, CHUNK), CHUNK)
        pick_t[:, rows] = jnp.transpose(pick[rows, :])

    codes_t = jnp.transpose(columns[...]).astype(jnp.int32)
    for n in range(BUCKETS):
        t, b = n // 4, n % 4
        code = columns[:, n : n + 1].astype(jnp.int32)
        gather[pl.ds(n * BUCKET, BUCKET), :] = onehot(iota((BUCKET, TROWS), 1) == code)
        gather_t[t, :, pl.ds(b * BUCKET, BUCKET)] = onehot(iota((TROWS, BUCKET), 0) == codes_t[n : n + 1, :])

    packed_row = iota((TABLES * TCHUNK, CHUNK), 0)
    within = packed_row % TCHUNK
    split = onehot(
        iota((TABLES * TCHUNK, CHUNK), 1) == SLOT * (within // CAP) + CAP * (packed_row // TCHUNK) + within % CAP
    )
    packed_lane = iota((CHUNK, TABLES * TCHUNK), 1)
    within = packed_lane % TCHUNK
    merge = onehot(
        iota((CHUNK, TABLES * TCHUNK), 0) == SLOT * (within // CAP) + CAP * (packed_lane // TCHUNK) + within % CAP
    )

    tail_row = iota((PER * TAIL, TABLES * TCHUNK), 0)
    within = iota((PER * TAIL, TABLES * TCHUNK), 1) % TCHUNK
    source_row = SLOT * (within // CAP) + CAP * (iota((PER * TAIL, TABLES * TCHUNK), 1) // TCHUNK) + within % CAP
    tail_row = SLOT * (tail_row // TAIL) + tail_row % TAIL
    merge_tail = jnp.concatenate([onehot(tail_row == source_row), onehot(tail_row + TAIL == source_row)], axis=0)

    scale = HEAD_DIM**-0.5
    log2e = 1.4426950408889634
    feature = iota((BUCKET, GF), 1) // HEAD_DIM
    heads = [onehot(feature == h) for h in range(GH)]
    term_heads = onehot(iota((24, GH * BUCKET), 0) % 8 == iota((24, GH * BUCKET), 1) // BUCKET)

    def attend(g, n):
        span = pl.ds(pl.multiple_of(n * BUCKET, BUCKET), BUCKET)
        tile = tiles[span, :]
        full = tile.astype(F32)
        turned = jnp.transpose(full)
        q_low, k_low, v_low, g_low = (tile[:, i * GF : (i + 1) * GF] for i in range(4))
        k_full = full[:, GF : 2 * GF]
        q_t, k_t, v_t, g_t = (turned[i * GF : (i + 1) * GF] for i in range(4))

        def spread_t(part):
            blocks = []
            for h in range(GH):
                pieces = [part[h * HEAD_DIM : (h + 1) * HEAD_DIM]]
                if h > 0:
                    pieces = [jnp.zeros((h * HEAD_DIM, BUCKET), F32)] + pieces
                if h < GH - 1:
                    pieces = pieces + [jnp.zeros(((GH - 1 - h) * HEAD_DIM, BUCKET), F32)]
                blocks.append(jnp.concatenate(pieces, axis=0))
            return jnp.concatenate(blocks, axis=1).astype(BF16)

        norms = jnp.concatenate(
            [
                -0.5 * jnp.sum(k_t[h * HEAD_DIM : (h + 1) * HEAD_DIM] ** 2, axis=0, keepdims=True)
                for h in range(GH)
            ]
            + [jnp.zeros((8 - GH, BUCKET), F32)],
            axis=0,
        )
        terms = []
        for _ in range(3):
            terms.append(norms.astype(BF16).astype(F32))
            norms = norms - terms[-1]
        terms = jnp.transpose(jnp.concatenate(terms, axis=0)).astype(BF16)
        keys = jnp.concatenate([k_low, terms], axis=1)
        queries = jnp.concatenate([spread_t(q_t), term_heads], axis=0)
        cotangents = spread_t(g_t)
        v_t_low, k_t_low = v_t.astype(BF16), k_t.astype(BF16)
        sums = jnp.zeros((BUCKET, GF), F32)
        key_sum, value_sum, query_rows = 0.0, 0.0, []
        yield
        for u in range(GH // 2):
            wide = slice(2 * BUCKET * u, 2 * BUCKET * (u + 1))
            narrow = slice(2 * HEAD_DIM * u, 2 * HEAD_DIM * (u + 1))
            logits = dot(keys, queries[:, wide])
            dprob = dot(v_low, cotangents[:, wide])
            yield
            top = jnp.max(logits, axis=0, keepdims=True)
            expons = jnp.exp2((logits - top) * (scale * log2e))
            probs = expons * (1.0 / jnp.sum(expons, axis=0, keepdims=True))
            probs_low = probs.astype(BF16)
            yield
            both = dot(v_t_low[narrow], probs_low)
            outputs = (both[:HEAD_DIM, :BUCKET], both[HEAD_DIM:, BUCKET:])
            delta = jnp.concatenate(
                [
                    jnp.sum(part * g_t[(2 * u + i) * HEAD_DIM : (2 * u + i + 1) * HEAD_DIM], axis=0, keepdims=True)
                    for i, part in enumerate(outputs)
                ],
                axis=1,
            )
            value_sum = value_sum + dot(
                probs_low, jnp.concatenate([g_low * heads[2 * u], g_low * heads[2 * u + 1]], axis=0)
            )
            yield
            dscore = scale * probs * (dprob - delta)
            dscore_low = dscore.astype(BF16)
            for i in range(2):
                total = jnp.sum(dscore[:, i * BUCKET : (i + 1) * BUCKET], axis=1, keepdims=True)
                sums = jnp.where(feature == 2 * u + i, total, sums)
            yield
            both = dot(k_t_low[narrow], dscore_low)
            query_rows += [both[:HEAD_DIM, :BUCKET], both[HEAD_DIM:, BUCKET:]]
            key_sum = key_sum + dot(
                dscore_low, jnp.concatenate([q_low * heads[2 * u], q_low * heads[2 * u + 1]], axis=0)
            )
        query_part = jnp.transpose(jnp.concatenate(query_rows, axis=0)).astype(BF16)
        key_part = (key_sum - sums * k_full).astype(BF16)
        value_part = value_sum.astype(BF16)
        grads[g][span, 0:256] = jnp.concatenate([query_part, key_part, value_part[:, :64]], axis=1)
        at = 256 + 32 * (1 - g)
        grads1[span, at : at + 32] = value_part[:, 64:]
        grads1[span, at + 64 : at + 96] = value_part[:, 64:]

    for g in range(GROUPS):
        wait_all(ins[g].at[pl.ds(SLOT, ROWS - SLOT)], recv_sem.at[CHUNKS + g])
        for k in range(CHUNKS):
            part = dot(split, ins[g][pl.ds(k * CHUNK, CHUNK), :]).astype(BF16)
            for t in range(TABLES):
                rows_of[t, pl.ds(k * TCHUNK, TCHUNK), :] = part[t * TCHUNK : (t + 1) * TCHUNK]
        for t in range(TABLES):
            rows = pl.ds(t * POINTS, POINTS)
            tiles[rows, :] = dot(gather[rows, :], rows_of[t]).astype(BF16)

        @pl.loop(0, BUCKETS // TOGETHER)
        def _(n, g=g):
            running = [attend(g, n * TOGETHER + i) for i in range(TOGETHER)]
            while running:
                running = [r for r in running if next(r, 0) is None]

        for t in range(TABLES):
            slots[g][t] = dot(gather_t[t], grads[g][pl.ds(t * POINTS, POINTS), :]).astype(BF16)
        for k in range(CHUNKS):
            part = jnp.concatenate([slots[g][t, pl.ds(k * TCHUNK, TCHUNK), :] for t in range(TABLES)], axis=0)
            backs[g][pl.ds(k * CHUNK, CHUNK), :] = dot(merge, part[:, :BACK]).astype(BF16)
            received = CHUNKS + GROUPS + k // (CHUNKS // PARTS)
            send(backs[g], homes[g], k, -1, 3 + g, received + g * PARTS)
            if g == 1:
                both = dot(merge_tail, part[:, BACK:])
                tail = jnp.where(iota((PER * TAIL, 128), 1) < 64, both[: PER * TAIL], both[PER * TAIL :])
                tail_back[pl.ds(k * PER, PER)] = tail.reshape(PER, TAIL, 128).astype(BF16)
                for step in range(max(1, k * PER), (k + 1) * PER):
                    copy(tail_back.at[step], tail_home.at[step], step, -1, 5, received + 2 * PARTS).start()
                if k == 0:
                    tail_home[0] = tail_back[0]

    part = ROWS // PARTS
    tails = part // 2
    wide = onehot(
        iota((part, tails), 1) == TAIL * (iota((part, tails), 0) // SLOT) + iota((part, tails), 0) % TAIL
    )
    own_half = (iota((part, 128), 0) % SLOT < TAIL) == (iota((part, 128), 1) < 64)
    for g in range(GROUPS):
        total = jnp.zeros((POINTS, GRADS[g]), F32)
        for p in range(PARTS):
            first = SLOT * (p == 0)
            received = CHUNKS + GROUPS + p
            wait_all(homes[g].at[pl.ds(p * part + first, part - first)], recv_sem.at[received + g * PARTS])
            rows = homes[g][pl.ds(p * part, part), :]
            if g == 1:
                owners = part // SLOT
                first = int(p == 0)
                wait_all(tail_home.at[pl.ds(p * owners + first, owners - first)], recv_sem.at[received + 2 * PARTS])
                tail = tail_home[pl.ds(p * owners, owners)].astype(F32).reshape(tails, 128).astype(BF16)
                rows = jnp.concatenate([rows, jnp.where(own_half, dot(wide, tail), 0.0).astype(BF16)], axis=1)
            total = total + dot(pick_t[:, p * part : (p + 1) * part], rows)
        result = jnp.transpose(total)
        for i in range(2):
            result_ref[pl.ds(i * FEAT + g * GF, GF), :] = result[i * GF : (i + 1) * GF].astype(BF16)
        result_ref[pl.ds(2 * FEAT + g * GF, 64), :] = result[192:256].astype(BF16)
    last = (result[256:320] + result[320:384]).astype(BF16)
    result_ref[pl.ds(2 * FEAT + GF + 64, 32), :] = last[:32]
    result_ref[pl.ds(2 * FEAT + 64, 32), :] = last[32:]

    wait_all(wanted.at[pl.ds(1, OWNERS - 1)], send_sem.at[0])
    for g in range(GROUPS):
        wait_all(outs[g].at[pl.ds(SLOT, ROWS - SLOT)], send_sem.at[1 + g])
        wait_all(backs[g].at[pl.ds(SLOT, ROWS - SLOT)], send_sem.at[3 + g])
    wait_all(tail_back.at[pl.ds(1, OWNERS - 1)], send_sem.at[5])


def divide(result_ref, query_out, key_out, value_out):
    for i, out in enumerate((query_out, key_out, value_out)):
        out[...] = result_ref[pl.ds(i * FEAT, FEAT), :]


def on_device(query, key_rows, value, out_grad, members):
    shape = jax.ShapeDtypeStruct(query.shape, BF16)
    vmem = pl.BlockSpec(memory_space=pltpu.VMEM)
    result = pl.pallas_call(
        kernel,
        name="hept_backward",
        out_shape=jax.ShapeDtypeStruct((3 * FEAT, POINTS), BF16),
        in_specs=[pl.BlockSpec(memory_space=pl.ANY)] * 5,
        out_specs=vmem,
        scratch_shapes=[
            *[pltpu.VMEM(query.shape, BF16)] * 4,
            pltpu.VMEM(members.shape, jnp.int32),
            *[pltpu.VMEM((128, 128), F32)] * 3,
            *[pltpu.VMEM((POINTS, WIDE), BF16)] * 2,
            pltpu.VMEM((ROWS, POINTS), BF16),
            pltpu.VMEM((POINTS, ROWS), BF16),
            pltpu.VMEM((BUCKETS * BUCKET, TROWS), BF16),
            pltpu.VMEM((TABLES, TROWS, POINTS), BF16),
            *[pltpu.VMEM((ROWS, WIDE), BF16)] * 4,
            pltpu.VMEM((TABLES, TROWS, WIDE), BF16),
            pltpu.VMEM((BUCKETS * BUCKET, WIDE), BF16),
            *[pltpu.VMEM((BUCKETS * BUCKET, width), BF16) for width in GRADS],
            *[pltpu.VMEM((TABLES, TROWS, width), BF16) for width in GRADS],
            *[pltpu.VMEM((ROWS, BACK), BF16)] * 4,
            *[pltpu.VMEM((OWNERS, TAIL, 128), BF16)] * 2,
            pltpu.SemaphoreType.DMA((5,)),
            pltpu.SemaphoreType.DMA((6,)),
            pltpu.SemaphoreType.DMA((CHUNKS + GROUPS + 3 * PARTS,)),
        ],
        compiler_params=pltpu.CompilerParams(
            collective_id=0, has_side_effects=True, vmem_limit_bytes=56 * 1024 * 1024
        ),
    )(query, key_rows, value, out_grad, members)
    return pl.pallas_call(
        divide, name="divide", out_shape=(shape,) * 3, in_specs=[vmem], out_specs=(vmem,) * 3
    )(result)


def solution(mesh):
    in_specs = (
        P(None, ("phi", "eta")),
        P(None, ("phi", "eta")),
        P(None, ("phi", "eta")),
        P(None, ("phi", "eta")),
        P(None, ("phi", "eta"), None),
    )
    out_specs = (P(None, ("phi", "eta")), P(None, ("phi", "eta")), P(None, ("phi", "eta")))
    return jax.shard_map(
        on_device, mesh=mesh, in_specs=in_specs, out_specs=out_specs, check_vma=False
    )
```

```python
import functools

import jax
import jax.numpy as jnp
from jax import lax
from jax.experimental import pallas as pl
from jax.experimental.pallas import tpu as pltpu
from jax.sharding import PartitionSpec as P

HEADS = 8
HEAD_DIM = 24
TABLES = 3
BUCKET = 128
BUCKETS = 12
POINTS = 512
OWNERS = 128
CAP = 5
SLOT = 16
ROWS = OWNERS * SLOT
TROWS = OWNERS * CAP
GROUPS = 2
GH = HEADS // GROUPS
GF = GH * HEAD_DIM
WIDE = 4 * GF
FEAT = HEADS * HEAD_DIM
GRADS = (256, 384)
BACK = 256
TAIL = SLOT // 2
CHUNK = 256
CHUNKS = ROWS // CHUNK
PER = CHUNK // SLOT
TCHUNK = PER * CAP
TOGETHER = 4
PARTS = 4


def hops(shift):
    return sum((0, 1, 2, 1)[shift // n % 4] for n in (32, 4, 1))


ORDER = [0] + sorted(((j * 37) % OWNERS for j in range(1, OWNERS)), key=hops)
MESH = pl.DeviceIdType.MESH
F32 = jnp.float32
BF16 = jnp.bfloat16


def dot(a, b):
    return jnp.dot(a, b, preferred_element_type=F32)


def iota(shape, dim):
    return lax.broadcasted_iota(jnp.int32, shape, dim)


def place():
    phi, eta = lax.axis_index("phi"), lax.axis_index("eta")
    return phi // 2, phi % 2, eta // 4, eta % 4


def torus():
    x, core, z, y = place()
    xs = [((x + a) % 4) * 2 for a in range(4)]
    cores = [core, 1 - core]
    zs = [((z + a) % 4) * 4 for a in range(4)]
    ys = [(y + a) % 4 for a in range(4)]

    def peer(step, sign):
        shift = ORDER[step]
        a, c, d = (sign * (shift // n) % 4 for n in (32, 4, 1))
        return (xs[a] + cores[shift // 16 % 2], zs[c] + ys[d])

    return peer


def onehot(mask):
    return jnp.where(mask, 1.0, 0.0).astype(BF16)


def kernel(
    query_any, key_any, value_any, grad_any, members_any,
    result_ref,
    query_ref, key_ref, value_ref, grad_ref, members_ref,
    columns, wanted, requests, points0, points1, pick, pick_t, gather, gather_t,
    out0, out1, in0, in1, rows_of, tiles, grads0, grads1, slots0, slots1, back0, back1, home0, home1, tail_back, tail_home,
    load_sem, send_sem, recv_sem,
):
    points_in, outs, ins = (points0, points1), (out0, out1), (in0, in1)
    grads, slots, backs, homes = (grads0, grads1), (slots0, slots1), (back0, back1), (home0, home1)
    peer = torus()

    def copy(src, dst, step, sign, sent, received):
        return pltpu.make_async_remote_copy(
            src_ref=src, dst_ref=dst, send_sem=send_sem.at[sent], recv_sem=recv_sem.at[received],
            device_id=peer(step, sign), device_id_type=MESH,
        )

    def wait_all(ref, sem):
        pltpu.make_async_copy(ref, ref, sem).wait()

    barrier = pltpu.get_barrier_semaphore()
    loads = [
        pltpu.make_async_copy(src, dst, load_sem.at[i])
        for i, (src, dst) in enumerate(
            [
                (members_any, members_ref),
                (query_any, query_ref),
                (key_any, key_ref),
                (value_any, value_ref),
                (grad_any, grad_ref),
            ]
        )
    ]
    loads[0].start()
    for step in range(1, OWNERS):
        pl.semaphore_signal(barrier, inc=1, device_id=peer(step, 1), device_id_type=MESH)
    for load in loads[1:]:
        load.start()
    loads[0].wait()

    x, core, z, y = place()
    ids = jnp.concatenate([members_ref[t] for t in range(TABLES)] + [jnp.zeros((4, 128), jnp.int32)], axis=0)
    source, local = ids >> 9, ids & 511
    shift = (
        (((x - (source >> 5)) & 3) << 5)
        | (((core - (source >> 4)) & 1) << 4)
        | (((z - (source >> 2)) & 3) << 2)
        | ((y - source) & 3)
    )
    step_of = jnp.zeros_like(shift)
    for step in range(1, OWNERS):
        step_of = jnp.where(shift == ORDER[step], step, step_of)
    both = (step_of * 1024 + local).astype(F32)
    columns[...] = jnp.transpose(jnp.concatenate([both, jnp.zeros((112, 128), F32)], axis=0))
    lane = iota((128, 128), 1)
    sub = iota((128, 128), 0)
    below = onehot(lane < sub)
    asked = jnp.zeros((128, 128), F32)
    codes = jnp.zeros((128, 128), F32)
    for t in range(TABLES):
        seen = jnp.zeros((1, 128), F32)
        for b in range(4):
            n = 4 * t + b
            column = columns[:, n : n + 1].astype(jnp.int32)
            step_col, ask = column >> 10, (column & 1023) + 1
            mine = lane == step_col
            mine_f = jnp.where(mine, 1.0, 0.0)
            earlier = dot(below, mine_f.astype(BF16)) + seen
            rank = jnp.sum(jnp.where(mine, earlier, 0.0), axis=1, keepdims=True).astype(jnp.int32)
            seen = seen + jnp.sum(mine_f, axis=0, keepdims=True)
            slot = CAP * t + rank
            asks = jnp.where(lane == slot, ask >> 4, 0) + jnp.where(lane == slot + SLOT, ask & 15, 0)
            mine_t = onehot(sub == step_of[n : n + 1, :])
            asked = asked + dot(mine_t, asks.astype(F32).astype(BF16))
            codes = jnp.where(lane == n, (CAP * step_col + rank).astype(F32), codes)
    wanted[...] = asked
    columns[...] = codes

    pl.semaphore_wait(barrier, OWNERS - 1)

    for step in range(1, OWNERS):
        row = pl.ds(step, 1)
        copy(wanted.at[row], requests.at[row], step, -1, 0, step // PER).start()
    requests[pl.ds(0, 1), :] = asked[0:1, :]
    for load in loads[1:]:
        load.wait()

    def turn_points(g):
        rows = pl.ds(g * GF, GF)
        stacked = jnp.concatenate([r[rows, :] for r in (query_ref, key_ref, value_ref, grad_ref)], axis=0)
        points_in[g][...] = jnp.transpose(stacked)

    chunk_row = iota((CHUNK, 128), 0)
    chunk_lane = iota((CHUNK, 128), 1)
    weight = jnp.where(chunk_lane == chunk_row % SLOT, 16.0, 0.0) + jnp.where(chunk_lane == chunk_row % SLOT + SLOT, 1.0, 0.0)
    spread = onehot(iota((CHUNK, PER), 1) == iota((CHUNK, PER), 0) // SLOT)
    ones = jnp.ones((128, POINTS), BF16)
    number = (iota((CHUNK, POINTS), 1) + 1).astype(F32)

    def send(src, dst, k, sign, number, received):
        for step in range(max(1, k * PER), (k + 1) * PER):
            rows = pl.ds(step * SLOT, SLOT)
            copy(src.at[rows], dst.at[rows], step, sign, number, received).start()
        if k == 0:
            dst[pl.ds(0, SLOT), :] = src[pl.ds(0, SLOT), :]

    turn_points(0)
    for k in range(CHUNKS):
        rows = pl.ds(k * CHUNK, CHUNK)
        wait_all(requests.at[pl.ds(max(1, k * PER), PER - (k == 0))], recv_sem.at[k])
        asks = dot(spread, requests[pl.ds(k * PER, PER), :].astype(BF16)) * weight
        picked = onehot(dot(asks.astype(BF16), ones) == number)
        pick[rows, :] = picked
        out0[rows, :] = dot(picked, points0[...]).astype(BF16)
        send(out0, in0, k, 1, 1, CHUNKS + k)
    turn_points(1)
    for k in range(CHUNKS):
        rows = pl.ds(k * CHUNK, CHUNK)
        out1[rows, :] = dot(pick[rows, :], points1[...]).astype(BF16)
        send(out1, in1, k, 1, 2, 2 * CHUNKS + k)

    @pl.loop(0, CHUNKS)
    def _(k):
        rows = pl.ds(pl.multiple_of(k * CHUNK, CHUNK), CHUNK)
        pick_t[:, rows] = jnp.transpose(pick[rows, :])

    codes_t = jnp.transpose(columns[...]).astype(jnp.int32)
    for n in range(BUCKETS):
        t, b = n // 4, n % 4
        code = columns[:, n : n + 1].astype(jnp.int32)
        gather[pl.ds(n * BUCKET, BUCKET), :] = onehot(iota((BUCKET, TROWS), 1) == code)
        gather_t[t, :, pl.ds(b * BUCKET, BUCKET)] = onehot(iota((TROWS, BUCKET), 0) == codes_t[n : n + 1, :])

    packed_row = iota((TABLES * TCHUNK, CHUNK), 0)
    within = packed_row % TCHUNK
    split = onehot(
        iota((TABLES * TCHUNK, CHUNK), 1) == SLOT * (within // CAP) + CAP * (packed_row // TCHUNK) + within % CAP
    )
    packed_lane = iota((CHUNK, TABLES * TCHUNK), 1)
    within = packed_lane % TCHUNK
    merge = onehot(
        iota((CHUNK, TABLES * TCHUNK), 0) == SLOT * (within // CAP) + CAP * (packed_lane // TCHUNK) + within % CAP
    )

    tail_row = iota((PER * TAIL, TABLES * TCHUNK), 0)
    within = iota((PER * TAIL, TABLES * TCHUNK), 1) % TCHUNK
    source_row = SLOT * (within // CAP) + CAP * (iota((PER * TAIL, TABLES * TCHUNK), 1) // TCHUNK) + within % CAP
    tail_row = SLOT * (tail_row // TAIL) + tail_row % TAIL
    merge_tail = jnp.concatenate([onehot(tail_row == source_row), onehot(tail_row + TAIL == source_row)], axis=0)

    scale = HEAD_DIM**-0.5
    log2e = 1.4426950408889634
    feature = iota((BUCKET, GF), 1) // HEAD_DIM
    heads = [onehot(feature == h) for h in range(GH)]
    term_heads = onehot(iota((24, GH * BUCKET), 0) % 8 == iota((24, GH * BUCKET), 1) // BUCKET)

    def attend(g, n):
        span = pl.ds(pl.multiple_of(n * BUCKET, BUCKET), BUCKET)
        tile = tiles[span, :]
        full = tile.astype(F32)
        turned = jnp.transpose(full)
        q_low, k_low, v_low, g_low = (tile[:, i * GF : (i + 1) * GF] for i in range(4))
        k_full = full[:, GF : 2 * GF]
        q_t, k_t, v_t, g_t = (turned[i * GF : (i + 1) * GF] for i in range(4))

        def spread_t(part):
            blocks = []
            for h in range(GH):
                pieces = [part[h * HEAD_DIM : (h + 1) * HEAD_DIM]]
                if h > 0:
                    pieces = [jnp.zeros((h * HEAD_DIM, BUCKET), F32)] + pieces
                if h < GH - 1:
                    pieces = pieces + [jnp.zeros(((GH - 1 - h) * HEAD_DIM, BUCKET), F32)]
                blocks.append(jnp.concatenate(pieces, axis=0))
            return jnp.concatenate(blocks, axis=1).astype(BF16)

        norms = jnp.concatenate(
            [
                -0.5 * jnp.sum(k_t[h * HEAD_DIM : (h + 1) * HEAD_DIM] ** 2, axis=0, keepdims=True)
                for h in range(GH)
            ]
            + [jnp.zeros((8 - GH, BUCKET), F32)],
            axis=0,
        )
        terms = []
        for _ in range(3):
            terms.append(norms.astype(BF16).astype(F32))
            norms = norms - terms[-1]
        terms = jnp.transpose(jnp.concatenate(terms, axis=0)).astype(BF16)
        keys = jnp.concatenate([k_low, terms], axis=1)
        queries = jnp.concatenate([spread_t(q_t), term_heads], axis=0)
        cotangents = spread_t(g_t)
        v_t_low, k_t_low = v_t.astype(BF16), k_t.astype(BF16)
        sums = jnp.zeros((BUCKET, GF), F32)
        key_sum, value_sum, query_rows = 0.0, 0.0, []
        yield
        for u in range(GH // 2):
            wide = slice(2 * BUCKET * u, 2 * BUCKET * (u + 1))
            narrow = slice(2 * HEAD_DIM * u, 2 * HEAD_DIM * (u + 1))
            logits = dot(keys, queries[:, wide])
            dprob = dot(v_low, cotangents[:, wide])
            yield
            top = jnp.max(logits, axis=0, keepdims=True)
            expons = jnp.exp2((logits - top) * (scale * log2e))
            probs = expons * (1.0 / jnp.sum(expons, axis=0, keepdims=True))
            probs_low = probs.astype(BF16)
            yield
            both = dot(v_t_low[narrow], probs_low)
            outputs = (both[:HEAD_DIM, :BUCKET], both[HEAD_DIM:, BUCKET:])
            delta = jnp.concatenate(
                [
                    jnp.sum(part * g_t[(2 * u + i) * HEAD_DIM : (2 * u + i + 1) * HEAD_DIM], axis=0, keepdims=True)
                    for i, part in enumerate(outputs)
                ],
                axis=1,
            )
            value_sum = value_sum + dot(
                probs_low, jnp.concatenate([g_low * heads[2 * u], g_low * heads[2 * u + 1]], axis=0)
            )
            yield
            dscore = scale * probs * (dprob - delta)
            dscore_low = dscore.astype(BF16)
            for i in range(2):
                total = jnp.sum(dscore[:, i * BUCKET : (i + 1) * BUCKET], axis=1, keepdims=True)
                sums = jnp.where(feature == 2 * u + i, total, sums)
            yield
            both = dot(k_t_low[narrow], dscore_low)
            query_rows += [both[:HEAD_DIM, :BUCKET], both[HEAD_DIM:, BUCKET:]]
            key_sum = key_sum + dot(
                dscore_low, jnp.concatenate([q_low * heads[2 * u], q_low * heads[2 * u + 1]], axis=0)
            )
        query_part = jnp.transpose(jnp.concatenate(query_rows, axis=0)).astype(BF16)
        key_part = (key_sum - sums * k_full).astype(BF16)
        value_part = value_sum.astype(BF16)
        grads[g][span, 0:256] = jnp.concatenate([query_part, key_part, value_part[:, :64]], axis=1)
        at = 256 + 32 * (1 - g)
        grads1[span, at : at + 32] = value_part[:, 64:]
        grads1[span, at + 64 : at + 96] = value_part[:, 64:]

    for g in range(GROUPS):
        for k in range(CHUNKS):
            first = SLOT * (k == 0)
            wait_all(ins[g].at[pl.ds(k * CHUNK + first, CHUNK - first)], recv_sem.at[(1 + g) * CHUNKS + k])
            part = dot(split, ins[g][pl.ds(k * CHUNK, CHUNK), :]).astype(BF16)
            for t in range(TABLES):
                rows_of[t, pl.ds(k * TCHUNK, TCHUNK), :] = part[t * TCHUNK : (t + 1) * TCHUNK]
        for t in range(TABLES):
            rows = pl.ds(t * POINTS, POINTS)
            tiles[rows, :] = dot(gather[rows, :], rows_of[t]).astype(BF16)

        @pl.loop(0, BUCKETS // TOGETHER)
        def _(n, g=g):
            running = [attend(g, n * TOGETHER + i) for i in range(TOGETHER)]
            while running:
                running = [r for r in running if next(r, 0) is None]

        for t in range(TABLES):
            slots[g][t] = dot(gather_t[t], grads[g][pl.ds(t * POINTS, POINTS), :]).astype(BF16)
        for k in range(CHUNKS):
            part = jnp.concatenate([slots[g][t, pl.ds(k * TCHUNK, TCHUNK), :] for t in range(TABLES)], axis=0)
            backs[g][pl.ds(k * CHUNK, CHUNK), :] = dot(merge, part[:, :BACK]).astype(BF16)
            received = 3 * CHUNKS + k // (CHUNKS // PARTS)
            send(backs[g], homes[g], k, -1, 3 + g, received + g * PARTS)
            if g == 1:
                both = dot(merge_tail, part[:, BACK:])
                tail = jnp.where(iota((PER * TAIL, 128), 1) < 64, both[: PER * TAIL], both[PER * TAIL :])
                tail_back[pl.ds(k * PER, PER)] = tail.reshape(PER, TAIL, 128).astype(BF16)
                for step in range(max(1, k * PER), (k + 1) * PER):
                    copy(tail_back.at[step], tail_home.at[step], step, -1, 5, received + 2 * PARTS).start()
                if k == 0:
                    tail_home[0] = tail_back[0]

    part = ROWS // PARTS
    tails = part // 2
    wide = onehot(
        iota((part, tails), 1) == TAIL * (iota((part, tails), 0) // SLOT) + iota((part, tails), 0) % TAIL
    )
    own_half = (iota((part, 128), 0) % SLOT < TAIL) == (iota((part, 128), 1) < 64)
    for g in range(GROUPS):
        total = jnp.zeros((POINTS, GRADS[g]), F32)
        for p in range(PARTS):
            first = SLOT * (p == 0)
            received = 3 * CHUNKS + p
            wait_all(homes[g].at[pl.ds(p * part + first, part - first)], recv_sem.at[received + g * PARTS])
            rows = homes[g][pl.ds(p * part, part), :]
            if g == 1:
                owners = part // SLOT
                first = int(p == 0)
                wait_all(tail_home.at[pl.ds(p * owners + first, owners - first)], recv_sem.at[received + 2 * PARTS])
                tail = tail_home[pl.ds(p * owners, owners)].astype(F32).reshape(tails, 128).astype(BF16)
                rows = jnp.concatenate([rows, jnp.where(own_half, dot(wide, tail), 0.0).astype(BF16)], axis=1)
            total = total + dot(pick_t[:, p * part : (p + 1) * part], rows)
        result = jnp.transpose(total)
        for i in range(2):
            result_ref[pl.ds(i * FEAT + g * GF, GF), :] = result[i * GF : (i + 1) * GF].astype(BF16)
        result_ref[pl.ds(2 * FEAT + g * GF, 64), :] = result[192:256].astype(BF16)
    last = (result[256:320] + result[320:384]).astype(BF16)
    result_ref[pl.ds(2 * FEAT + GF + 64, 32), :] = last[:32]
    result_ref[pl.ds(2 * FEAT + 64, 32), :] = last[32:]

    wait_all(wanted.at[pl.ds(1, OWNERS - 1)], send_sem.at[0])
    for g in range(GROUPS):
        wait_all(outs[g].at[pl.ds(SLOT, ROWS - SLOT)], send_sem.at[1 + g])
        wait_all(backs[g].at[pl.ds(SLOT, ROWS - SLOT)], send_sem.at[3 + g])
    wait_all(tail_back.at[pl.ds(1, OWNERS - 1)], send_sem.at[5])


def divide(result_ref, query_out, key_out, value_out):
    for i, out in enumerate((query_out, key_out, value_out)):
        out[...] = result_ref[pl.ds(i * FEAT, FEAT), :]


def on_device(query, key_rows, value, out_grad, members):
    shape = jax.ShapeDtypeStruct(query.shape, BF16)
    vmem = pl.BlockSpec(memory_space=pltpu.VMEM)
    result = pl.pallas_call(
        kernel,
        name="hept_backward",
        out_shape=jax.ShapeDtypeStruct((3 * FEAT, POINTS), BF16),
        in_specs=[pl.BlockSpec(memory_space=pl.ANY)] * 5,
        out_specs=vmem,
        scratch_shapes=[
            *[pltpu.VMEM(query.shape, BF16)] * 4,
            pltpu.VMEM(members.shape, jnp.int32),
            *[pltpu.VMEM((128, 128), F32)] * 3,
            *[pltpu.VMEM((POINTS, WIDE), BF16)] * 2,
            pltpu.VMEM((ROWS, POINTS), BF16),
            pltpu.VMEM((POINTS, ROWS), BF16),
            pltpu.VMEM((BUCKETS * BUCKET, TROWS), BF16),
            pltpu.VMEM((TABLES, TROWS, POINTS), BF16),
            *[pltpu.VMEM((ROWS, WIDE), BF16)] * 4,
            pltpu.VMEM((TABLES, TROWS, WIDE), BF16),
            pltpu.VMEM((BUCKETS * BUCKET, WIDE), BF16),
            *[pltpu.VMEM((BUCKETS * BUCKET, width), BF16) for width in GRADS],
            *[pltpu.VMEM((TABLES, TROWS, width), BF16) for width in GRADS],
            *[pltpu.VMEM((ROWS, BACK), BF16)] * 4,
            *[pltpu.VMEM((OWNERS, TAIL, 128), BF16)] * 2,
            pltpu.SemaphoreType.DMA((5,)),
            pltpu.SemaphoreType.DMA((6,)),
            pltpu.SemaphoreType.DMA((3 * CHUNKS + 3 * PARTS,)),
        ],
        compiler_params=pltpu.CompilerParams(
            collective_id=0, has_side_effects=True, vmem_limit_bytes=56 * 1024 * 1024
        ),
    )(query, key_rows, value, out_grad, members)
    return pl.pallas_call(
        divide, name="divide", out_shape=(shape,) * 3, in_specs=[vmem], out_specs=(vmem,) * 3
    )(result)


def solution(mesh):
    in_specs = (
        P(None, ("phi", "eta")),
        P(None, ("phi", "eta")),
        P(None, ("phi", "eta")),
        P(None, ("phi", "eta")),
        P(None, ("phi", "eta"), None),
    )
    out_specs = (P(None, ("phi", "eta")), P(None, ("phi", "eta")), P(None, ("phi", "eta")))
    return jax.shard_map(
        on_device, mesh=mesh, in_specs=in_specs, out_specs=out_specs, check_vma=False
    )
```
